128 devices in a mesh: ep: 32 (over z, y, core), rep: 4 (over x).
Axes of the slice: x: 4, y: 4, z: 4, core: 2. Of those that a mesh axis runs over, the one named last changes fastest.
Arguments:
- tokens: bfloat16 [16384, 2304], P(('ep', 'rep')), may hold values from -6 to 6
- output_grad: bfloat16 [16384, 2304], P(('ep', 'rep')), may hold values from -2 to 2
- chosen_experts: int32 [16384, 8], P(('ep', 'rep')), may hold values from 0 to 127, all different within a row; in each aligned block of 128 rows (0 to 127, 128 to 255, ...) at most 9 rows name the same one
- route_weights: float32 [16384, 8], P(('ep', 'rep')), may hold values from 0.1 to 0.5
- gate_weight: bfloat16 [128, 2304, 1024], P(('ep', 'rep')), may hold values from -0.125 to 0.125
- up_weight: bfloat16 [128, 2304, 1024], P(('ep', 'rep')), may hold values from -0.125 to 0.125
- down_weight: bfloat16 [128, 1024, 2304], P(('ep', 'rep')), may hold values from -0.1875 to 0.1875
- gate_adapter_in: bfloat16 [128, 16, 2304], P(('ep', 'rep')), may hold values from -0.125 to 0.125
- gate_adapter_out: bfloat16 [128, 16, 1024], P(('ep', 'rep')), may hold values from -1 to 1
- up_adapter_in: bfloat16 [128, 16, 2304], P(('ep', 'rep')), may hold values from -0.125 to 0.125
- up_adapter_out: bfloat16 [128, 16, 1024], P(('ep', 'rep')), may hold values from -1 to 1
- shared_gate: bfloat16 [2304, 512], P(None, 'rep'), may hold values from -0.125 to 0.125
- shared_up: bfloat16 [2304, 512], P(None, 'rep'), may hold values from -0.125 to 0.125
- shared_down: bfloat16 [2304, 512], P(None, 'rep'), may hold values from -0.25 to 0.25
Outputs:
- token_grad: bfloat16 [16384, 2304], P(('ep', 'rep'))
- gate_in_grad: float32 [128, 16, 2304], P(('ep', 'rep'))
- gate_out_grad: float32 [128, 16, 1024], P(('ep', 'rep'))
- up_in_grad: float32 [128, 16, 2304], P(('ep', 'rep'))
- up_out_grad: float32 [128, 16, 1024], P(('ep', 'rep'))
The draws below stay inside these ranges and needn't reach their ends.
Inputs may be any that keep to these rules, and one draw needn't show every extreme that they name: `chosen_experts`: each row names 8 different experts. In each aligned block of 128 rows no expert is named by more than 9 rows, and in some block an expert is named by exactly 9 rows.
All inputs are finite; a program needn't handle non-finite values.
Results may differ from the reference program's by a relative error of at most 0.0064.
Values may be sent and summed in bfloat16 or wider, within the bound.
A program may use at most 128 MiB of HBM per device.

```python
import math
import jax
import jax.numpy as jnp
import numpy as np
from jax import lax

D = 2304
FF = 1024
SFF = 512
RANK = 16
TOP = 8
TOK_DEV = 128
EXPERTS = 128
CAP = 9
TOKENS = 16384
N_EP = 32
N_REP = 4


def block_levels(key, extent, shards, low, largest):
    def one(dim, shards_of):
        steps = jax.random.uniform(jax.random.fold_in(jax.random.fold_in(key, 6), dim), (shards_of,), jnp.float32, low / len(shards), largest / len(shards))
        return jnp.repeat(jnp.exp(steps), extent[dim] // shards_of).reshape((-1,) + (1,) * (len(extent) - dim - 1))

    factor_of = one(*shards[0])
    for cut in shards[1:]:
        factor_of = factor_of * one(*cut)
    return factor_of


def assign_block(stream_key, own, number, rows, count, top, bound, slope):
    order = jax.random.permutation(stream_key, count)
    heavy_load, common = shares(count, rows * top, bound, slope, True), shares(count, rows * top, bound, slope, False)
    places = jnp.arange(count)

    def named(sizes, rotation):
        used = int((sizes > 0).sum())
        fixed = max(1, used // 4)
        moved = fixed + (places - fixed + rotation * (used - fixed)) % max(1, count - fixed)
        return jnp.zeros((count,), jnp.int32).at[order[jnp.where(places < fixed, places, moved)]].set(jnp.asarray(sizes, jnp.int32))

    sizes = jnp.where(number % 4 == 0, named(heavy_load, number // 4), named(common, number - number // 4 - 1))
    mixed = jax.random.permutation(jax.random.fold_in(own, 3), count)
    source_of, receiver = mixed[0:count // 2 * 2:2], mixed[1:count // 2 * 2:2]
    margin = jnp.minimum(sizes[source_of] - 1, bound - sizes[receiver]) // 2
    margin = jnp.where((source_of == order[0]) | (receiver == order[0]) | (sizes[receiver] == 0), 0, jnp.maximum(margin, 0))
    moved = jax.random.randint(jax.random.fold_in(own, 4), (count // 2,), 0, 1 << 20) % (margin + 1)
    sizes = sizes.at[source_of].add(-moved).at[receiver].add(moved)
    items = jnp.searchsorted(jnp.cumsum(sizes), jnp.arange(rows * top), side="right").astype(jnp.int32)
    grid = items.reshape(top, rows).T
    grid = grid[jax.random.permutation(jax.random.fold_in(own, 1), rows)]
    rotation = jax.random.randint(jax.random.fold_in(own, 2), (rows, 1), 0, top)
    return jnp.take_along_axis(grid, (jnp.arange(top)[None, :] + rotation) % top, axis=1)


def shares(number_of, total, bound, slope, full):
    portions = [(1 << 20) // math.isqrt(grade ** slope) + 1 for grade in range(1, number_of + 1)]
    largest = bound if full else min(bound, max(-(-total // number_of), total * portions[0] // sum(portions)))
    least = 1 if total - largest >= number_of - 1 else 0
    given, rest = [largest] + [least] * (number_of - 1), total - largest - least * (number_of - 1)
    while rest > 0:
        movable = [i for i in range(1, number_of) if given[i] < largest] or [i for i in range(1, number_of) if given[i] < bound]
        pool, budget = sum([portions[i] for i in movable]), rest
        for i in movable:
            more = min(bound - given[i], max(1, budget * portions[i] // pool), rest)
            given[i] = given[i] + more
            rest = rest - more
    return np.array(given)


def gaussian(own_key, extent, deviation, most, cuts=(), kind=jnp.bfloat16):
    factor_of = block_levels(own_key, extent, cuts, -0.22, 0.18) if cuts else 1.0
    values = jax.random.normal(own_key, extent, jnp.float32) * deviation * factor_of
    return jnp.minimum(jnp.maximum(values, -most), most).astype(kind)


def setup_inputs(seed: int = 0) -> dict:
    key_of = jax.random.split(jax.random.key(seed), 15)
    tokens = gaussian(key_of[0], (TOKENS, D), 1.0, 6.0, ((0, 128),))
    output_grad = gaussian(key_of[1], (TOKENS, D), 0.3, 2.0, ((0, 128),))
    chosen_experts_keys = jax.random.split(jax.random.fold_in(key_of[2], 1), TOKENS // TOK_DEV)
    chosen_experts_turns = jax.random.permutation(jax.random.fold_in(key_of[2], 3), TOKENS // TOK_DEV)
    chosen_experts = jax.vmap(lambda own, number: assign_block(jax.random.fold_in(key_of[2], 2), own, number, TOK_DEV, EXPERTS, TOP, CAP, 1))(chosen_experts_keys, chosen_experts_turns).reshape((TOKENS, TOP))
    route_weights = jnp.clip(0.1 + 0.4 * jax.random.uniform(key_of[3], (TOKENS, TOP), jnp.float32) ** block_levels(key_of[3], (TOKENS, TOP), ((0, 128),), -0.2, 0.2), 0.1, 0.5)
    gate_weight = gaussian(key_of[4], (EXPERTS, D, FF), D ** -0.5, 0.125, ((0, 128),))
    up_weight = gaussian(key_of[5], (EXPERTS, D, FF), D ** -0.5, 0.125, ((0, 128),))
    down_weight = gaussian(key_of[6], (EXPERTS, FF, D), FF ** -0.5, 0.1875, ((0, 128),))
    gate_adapter_in = gaussian(key_of[7], (EXPERTS, RANK, D), D ** -0.5, 0.125, ((0, 128),))
    gate_adapter_out = gaussian(key_of[8], (EXPERTS, RANK, FF), (2 * RANK) ** -0.5, 1.0, ((0, 128),))
    up_adapter_in = gaussian(key_of[9], (EXPERTS, RANK, D), D ** -0.5, 0.125, ((0, 128),))
    up_adapter_out = gaussian(key_of[10], (EXPERTS, RANK, FF), (2 * RANK) ** -0.5, 1.0, ((0, 128),))
    shared_gate = gaussian(key_of[11], (D, SFF), D ** -0.5, 0.125, ((1, 4),))
    shared_up = gaussian(key_of[12], (D, SFF), D ** -0.5, 0.125, ((1, 4),))
    shared_down = gaussian(key_of[13], (D, SFF), SFF ** -0.5, 0.25, ((1, 4),))
    return dict(tokens=tokens, output_grad=output_grad, chosen_experts=chosen_experts, route_weights=route_weights, gate_weight=gate_weight, up_weight=up_weight, down_weight=down_weight, gate_adapter_in=gate_adapter_in, gate_adapter_out=gate_adapter_out, up_adapter_in=up_adapter_in, up_adapter_out=up_adapter_out, shared_gate=shared_gate, shared_up=shared_up, shared_down=shared_down)


def contract_last(left, right):
    return lax.dot_general(left, right, (((1,), (1,)), ((), ())), preferred_element_type=jnp.float32)


def contract_first(left, right):
    return lax.dot_general(left, right, (((0,), (0,)), ((), ())), preferred_element_type=jnp.float32)


def expert_pass(input_rows, grad_rows, weights):
    gate_w, up_w, down_w, gate_in, gate_out, up_in, up_out = weights
    low_gate = contract_last(input_rows, gate_in).astype(jnp.bfloat16)
    low_up = contract_last(input_rows, up_in).astype(jnp.bfloat16)
    gate_pre = jnp.dot(input_rows, gate_w, preferred_element_type=jnp.float32) + jnp.dot(low_gate, gate_out, preferred_element_type=jnp.float32)
    up_pre = jnp.dot(input_rows, up_w, preferred_element_type=jnp.float32) + jnp.dot(low_up, up_out, preferred_element_type=jnp.float32)
    d_hidden = contract_last(grad_rows, down_w)
    gate_sigmoid = jax.nn.sigmoid(gate_pre)
    d_gate = (d_hidden * up_pre * gate_sigmoid * (1.0 + gate_pre * (1.0 - gate_sigmoid))).astype(jnp.bfloat16)
    d_up = (d_hidden * gate_pre * gate_sigmoid).astype(jnp.bfloat16)
    low_dgate = contract_last(d_gate, gate_out).astype(jnp.bfloat16)
    low_dup = contract_last(d_up, up_out).astype(jnp.bfloat16)
    row_grads = contract_last(d_gate, gate_w) + jnp.dot(low_dgate, gate_in, preferred_element_type=jnp.float32)
    row_grads = row_grads + contract_last(d_up, up_w) + jnp.dot(low_dup, up_in, preferred_element_type=jnp.float32)
    adapter_grads = (contract_first(low_dgate, input_rows), contract_first(low_gate, d_gate), contract_first(low_dup, input_rows), contract_first(low_up, d_up))
    return row_grads.astype(jnp.bfloat16), adapter_grads


def shared_pass(input_rows, grad_rows, gate_w, up_w, down_w):
    gate_pre = jnp.dot(input_rows, gate_w, preferred_element_type=jnp.float32)
    up_pre = jnp.dot(input_rows, up_w, preferred_element_type=jnp.float32)
    d_hidden = jnp.dot(grad_rows, down_w, preferred_element_type=jnp.float32)
    gate_sigmoid = jax.nn.sigmoid(gate_pre)
    d_gate = (d_hidden * up_pre * gate_sigmoid * (1.0 + gate_pre * (1.0 - gate_sigmoid))).astype(jnp.bfloat16)
    d_up = (d_hidden * gate_pre * gate_sigmoid).astype(jnp.bfloat16)
    return contract_last(d_gate, gate_w) + contract_last(d_up, up_w)


def reference(tokens, output_grad, chosen_experts, route_weights, gate_weight, up_weight, down_weight, gate_adapter_in, gate_adapter_out, up_adapter_in, up_adapter_out, shared_gate, shared_up, shared_down):
    pick_total = TOKENS * TOP
    room = N_EP * N_REP * CAP
    flat_experts = chosen_experts.reshape(pick_total)
    onehot = (flat_experts[:, None] == jnp.arange(EXPERTS, dtype=jnp.int32)[None, :]).astype(jnp.int32)
    position = jnp.sum((jnp.cumsum(onehot, axis=0) - onehot) * onehot, axis=1).astype(jnp.int32)
    table = jnp.full((EXPERTS, room), pick_total, jnp.int32).at[flat_experts, position].set(jnp.arange(pick_total, dtype=jnp.int32))
    owner_token = jnp.concatenate([jnp.arange(pick_total, dtype=jnp.int32) // TOP, jnp.full((1,), TOKENS, jnp.int32)])
    padded_tokens = jnp.concatenate([tokens, jnp.zeros((1, D), jnp.bfloat16)])
    padded_grads = jnp.concatenate([output_grad, jnp.zeros((1, D), jnp.bfloat16)])
    padded_weights = jnp.concatenate([route_weights.reshape(pick_total), jnp.zeros((1,), jnp.float32)])

    def expert_step(total, expert):
        pick_rows = table[expert]
        token_index = owner_token[pick_rows]
        input_rows = padded_tokens[token_index]
        grad_rows = (padded_weights[pick_rows][:, None] * padded_grads[token_index].astype(jnp.float32)).astype(jnp.bfloat16)
        weights = (gate_weight[expert], up_weight[expert], down_weight[expert], gate_adapter_in[expert], gate_adapter_out[expert], up_adapter_in[expert], up_adapter_out[expert])
        row_grads, adapter_grads = expert_pass(input_rows, grad_rows, weights)
        total = total.at[token_index].add(row_grads.astype(jnp.float32))
        return total, adapter_grads

    total, adapter_grads = lax.scan(expert_step, jnp.zeros((TOKENS + 1, D), jnp.float32), jnp.arange(EXPERTS, dtype=jnp.int32))
    shared_grad = shared_pass(tokens, output_grad, shared_gate, shared_up, shared_down)
    token_grad = (total[:TOKENS] + shared_grad).astype(jnp.bfloat16)
    return token_grad, adapter_grads[0], adapter_grads[1], adapter_grads[2], adapter_grads[3]
```

```python
import functools

import jax
import jax.numpy as jnp
import numpy as np
from jax import lax
from jax.experimental import pallas as pl
from jax.experimental.pallas import tpu as pltpu
from jax.sharding import PartitionSpec as P

MESH = pl.DeviceIdType.MESH
BF = jnp.bfloat16
F32 = jnp.float32

TD = 128
D = 2304
FF = 1024
CAP = 9
NB = 8
NPEER = 16
MSG = NB * CAP
ROWS = NPEER * MSG
GR = 4 * MSG
ND = 3
CW = D // ND
NP = 2 * ND
HALF = 4 * TD


def dot(a, b):
    return jnp.dot(a, b, preferred_element_type=F32)


def dot_last(a, b):
    return lax.dot_general(a, b, (((1,), (1,)), ((), ())), preferred_element_type=F32)


def dot_first(a, b):
    return lax.dot_general(a, b, (((0,), (0,)), ((), ())), preferred_element_type=F32)


def position():
    e, x = lax.axis_index("ep"), lax.axis_index("rep")
    return e // 8, (e // 2) % 4, e % 2, x


def peer(i, sign):
    z, y, c, x = position()
    oy = i % 4
    oz = (i % 4 + i // 4) % 4
    zz = (z + sign * oz + 4) % 4
    yy = (y + sign * oy + 4) % 4
    return {"ep": (zz * 4 + yy) * 2 + c, "rep": x}


def x_peer(o):
    z, y, c, x = position()
    return {"ep": (z * 4 + y) * 2 + c, "rep": (x + o) % 4}


def member(o):
    z, y, c, x = position()
    return {"ep": (z * 4 + y) * 2 + (c + o // 4) % 2, "rep": (x + o) % 4}


def member_slot(o):
    z, y, c, x = position()
    return ((c + o // 4) % 2) * 4 + (x + o) % 4


def sibling():
    z, y, c, x = position()
    return {"ep": (z * 4 + y) * 2 + 1 - c, "rep": x}


def remote(src, dst, send, recv, device):
    return pltpu.make_async_remote_copy(
        src_ref=src,
        dst_ref=dst,
        send_sem=send,
        recv_sem=recv,
        device_id=device,
        device_id_type=MESH,
    )


def wait_for(ref, sem):
    pltpu.make_async_copy(ref, ref, sem).wait()


def kernel(
    tok,
    grd,
    meta,
    expand,
    slot_of,
    block_of,
    block_row,
    gw_h,
    uw_h,
    dw_h,
    gin,
    gout,
    uin,
    uout,
    sg_h,
    su_h,
    sd_h,
    out,
    gin_g,
    gout_g,
    uin_g,
    uout_g,
    sb,
    rb,
    ob,
    ret,
    gw,
    uw,
    dw,
    sg,
    su,
    sd,
    meta_all,
    xg,
    place,
    place_t,
    wsl,
    tmp,
    stage,
    xb,
    gb,
    dg,
    du,
    outb,
    sga,
    sua,
    sda,
    sdg,
    sdu,
    retv,
    own,
    csb,
    crb,
    xsb,
    xrb,
    fin,
    w_sem,
    s_sem,
    m_send,
    m_recv,
    m_own,
    own_sem,
    gx_send,
    gx_recv,
    gc_send,
    gc_recv,
    st_sem,
    d_send,
    d_recv,
    d_own,
    in_sem,
    o_sem,
    r_send,
    r_recv,
    r_own,
    rv_sem,
    c_send,
    c_recv,
    x_send,
    x_recv,
    f_sem,
):
    z, y, c, x = position()
    me = c * 4 + x

    barrier = pltpu.get_barrier_semaphore()

    @pl.loop(1, NPEER)
    def _(i):
        pl.semaphore_signal(barrier, inc=1, device_id=peer(i, 1), device_id_type=MESH)

    @pl.loop(1, 8)
    def _(o):
        pl.semaphore_signal(barrier, inc=1, device_id=member(o), device_id_type=MESH)

    weights = [(gw_h, gw), (uw_h, uw), (dw_h, dw)]
    shared = [(sg_h, sg), (su_h, su), (sd_h, sd)]
    own_meta = pltpu.make_async_copy(meta.at[me], meta_all.at[me], m_own)
    own_meta.start()

    def own_piece(p):
        src = tok if p < ND else grd
        return pltpu.make_async_copy(
            src.at[:, pl.ds((p % ND) * CW, CW)],
            xg.at[p, pl.ds(me * TD, TD), :],
            own_sem.at[p],
        )

    for p in range(NP):
        own_piece(p).start()
    for h, v in shared:
        pltpu.make_async_copy(h, v, s_sem).start()
    for j, (h, v) in enumerate(weights):
        pltpu.make_async_copy(h, v, w_sem.at[j]).start()
    gin_g[...] = jnp.zeros_like(gin_g)
    gout_g[...] = jnp.zeros_like(gout_g)
    uin_g[...] = jnp.zeros_like(uin_g)
    uout_g[...] = jnp.zeros_like(uout_g)
    sga[...] = jnp.zeros_like(sga)
    sua[...] = jnp.zeros_like(sua)
    sda[...] = jnp.zeros_like(sda)

    pl.semaphore_wait(barrier, NPEER - 1 + 7)

    @pl.loop(1, 8)
    def _(o):
        remote(meta.at[member_slot(o)], meta_all.at[me], m_send, m_recv, member(o)).start()

    for p in range(NP):
        src = (tok if p < ND else grd).at[:, pl.ds((p % ND) * CW, CW)]
        dst = xg.at[p, pl.ds(me * TD, TD), :]
        for o in (1, 3, 2):
            remote(src, dst, gx_send, gx_recv.at[p, o - 1], x_peer(o)).start()
        remote(src, dst, gc_send, gc_recv.at[p], sibling()).start()

    own_meta.wait()
    wait_for(meta_all.at[pl.ds(0, 7)], m_recv)

    spread = expand[...]
    code = meta_all[:, 0].reshape(TD, TD).astype(BF)
    hit = jnp.where(dot(spread, code) == slot_of[...], 1.0, 0.0)
    w_all = meta_all[:, 1].reshape(TD, TD)
    w_hi = w_all.astype(BF)
    left = w_all - w_hi.astype(F32)
    w_mid = left.astype(BF)
    w_lo = (left - w_mid.astype(F32)).astype(BF)
    w_row = (dot(spread, w_hi) + dot(spread, w_mid)) + dot(spread, w_lo)
    wsl[...] = jnp.broadcast_to(jnp.sum(w_row * hit, axis=1, keepdims=True), (ROWS, TD))
    hit_t = hit.T
    for b in range(NB):
        place[:, b * TD : (b + 1) * TD] = jnp.where(block_of[...] == float(b), hit, 0.0).astype(BF)
        place_t[b * TD : (b + 1) * TD, :] = (hit_t * block_row[b : b + 1, :]).astype(BF)

    wait_shared = [pltpu.make_async_copy(h, v, s_sem) for h, v in shared]
    for cp in wait_shared:
        cp.wait()

    mine = pl.multiple_of(c * HALF, HALF)
    other = pl.multiple_of((1 - c) * HALF, HALF)

    def rows_of(k):
        return pl.ds(pl.multiple_of(k * GR, 8), GR)

    def send_piece(p, k, slot):
        cp = pltpu.make_async_copy(stage.at[slot], sb.at[p, rows_of(k), :], st_sem)
        cp.start()
        cp.wait()

        @pl.loop(0, 4)
        def _(j):
            i = k * 4 + j
            rows = pl.ds(pl.multiple_of(i * MSG, 8), MSG)

            @pl.when(i > 0)
            def _():
                remote(
                    sb.at[p, rows, :], rb.at[p, rows, :], d_send, d_recv.at[k], peer(i, 1)
                ).start()

            @pl.when(i == 0)
            def _():
                pltpu.make_async_copy(sb.at[p, rows, :], rb.at[p, rows, :], d_own).start()

    def scaled(acc, p, k):
        scale = jnp.where(p < ND, 1.0, wsl[rows_of(k), :][:, 0:1])
        return (acc * scale).astype(BF)

    def arrive(p):
        for o in (1, 3, 2):
            slot = pl.ds(pl.multiple_of((c * 4 + (x + 4 - o) % 4) * TD, TD), TD)
            block = xg.at[p, slot, :]
            wait_for(block, gx_recv.at[p, o - 1])
            remote(block, block, gc_send, gc_recv.at[p], sibling()).start()

    def first_groups(p, shared_part):
        arrive(p)

        @pl.loop(0, 2)
        def _(k):
            for n in range(3):
                cols = slice(n * 256, (n + 1) * 256)
                tmp[k, :, cols] = dot(
                    place[rows_of(k), pl.ds(mine, HALF)], xg[p, pl.ds(mine, HALF), cols]
                )

        wait_for(xg.at[p, pl.ds(other, HALF), :], gc_recv.at[p])

        @pl.loop(0, 2)
        def _(k):
            for n in range(3):
                cols = slice(n * 256, (n + 1) * 256)
                acc = tmp[k, :, cols] + dot(
                    place[rows_of(k), pl.ds(other, HALF)], xg[p, pl.ds(other, HALF), cols]
                )
                stage[k, :, cols] = scaled(acc, p, k)
            send_piece(p, k, k)

        shared_part(xg[p, pl.ds(mine, HALF), :])

    @pl.loop(0, ND)
    def _(d):
        pltpu.make_async_copy(
            tok.at[:, pl.ds(0, CW)], xg.at[d, pl.ds(me * TD, TD), :], own_sem.at[d]
        ).wait()
        rows = pl.ds(pl.multiple_of(d * CW, CW), CW)

        def part(block):
            sga[...] += dot(block, sg[rows, :])
            sua[...] += dot(block, su[rows, :])

        first_groups(d, part)

    @pl.loop(0, ND)
    def _(d):
        p = d + ND
        pltpu.make_async_copy(
            tok.at[:, pl.ds(0, CW)], xg.at[p, pl.ds(me * TD, TD), :], own_sem.at[p]
        ).wait()
        rows = pl.ds(pl.multiple_of(d * CW, CW), CW)

        def part(block):
            sda[...] += dot(block, sd[rows, :])

        first_groups(p, part)

    s_gate, s_up, s_hid = sga[...], sua[...], sda[...]
    sig = jax.nn.sigmoid(s_gate)
    sdg[...] = (s_hid * s_up * sig * (1.0 + s_gate * (1.0 - sig))).astype(BF)
    sdu[...] = (s_hid * s_gate * sig).astype(BF)

    for j, (h, v) in enumerate(weights):
        pltpu.make_async_copy(h, v, w_sem.at[j]).wait()

    def late_group(k):
        @pl.loop(0, NP)
        def _(p):
            for n in range(3):
                cols = slice(n * 256, (n + 1) * 256)
                acc = dot(place[rows_of(k), :], xg[p, :, cols])
                stage[0, :, cols] = scaled(acc, p, k)
            send_piece(p, k, 0)

    def fetch(k):
        for d in range(ND):
            pltpu.make_async_copy(rb.at[d, rows_of(k), :], xb.at[d], in_sem).start()
            pltpu.make_async_copy(rb.at[ND + d, rows_of(k), :], gb.at[d], in_sem).start()
        wait_for(xb, in_sem)
        wait_for(gb, in_sem)

    def expert(k):
        low_gate = sum(dot_last(xb[d], gin[:, d * CW : (d + 1) * CW]) for d in range(ND)).astype(BF)
        low_up = sum(dot_last(xb[d], uin[:, d * CW : (d + 1) * CW]) for d in range(ND)).astype(BF)

        @pl.loop(0, FF // 256)
        def _(j):
            cols = pl.ds(pl.multiple_of(j * 256, 256), 256)
            gate = sum(dot(xb[d], gw[d * CW : (d + 1) * CW, cols]) for d in range(ND))
            gate = gate + dot(low_gate, gout[:, cols])
            up = sum(dot(xb[d], uw[d * CW : (d + 1) * CW, cols]) for d in range(ND))
            up = up + dot(low_up, uout[:, cols])
            hid = sum(dot_last(gb[d], dw[cols, d * CW : (d + 1) * CW]) for d in range(ND))
            s = jax.nn.sigmoid(gate)
            dg[:, cols] = (hid * up * s * (1.0 + gate * (1.0 - s))).astype(BF)
            du[:, cols] = (hid * gate * s).astype(BF)

        dgv, duv = dg[...], du[...]
        low_dg = dot_last(dgv, gout[...]).astype(BF)
        low_du = dot_last(duv, uout[...]).astype(BF)
        gout_g[...] += dot_first(low_gate, dgv)
        uout_g[...] += dot_first(low_up, duv)
        for d in range(ND):
            cols = slice(d * CW, (d + 1) * CW)
            gin_g[:, cols] += dot_first(low_dg, xb[d])
            uin_g[:, cols] += dot_first(low_du, xb[d])

        @pl.loop(0, ND)
        def _(d):
            for n in range(3):
                rows = pl.ds(pl.multiple_of(d * CW + n * 256, 256), 256)
                acc = dot_last(dg[...], gw[rows, :]) + dot(low_dg, gin[:, rows])
                acc = acc + dot_last(du[...], uw[rows, :]) + dot(low_du, uin[:, rows])
                outb[d, :, n * 256 : (n + 1) * 256] = acc.astype(BF)

    def send_back(k):
        for d in range(ND):
            pltpu.make_async_copy(outb.at[d], ob.at[d, rows_of(k), :], o_sem).start()
        wait_for(outb, o_sem)

        @pl.loop(0, ND)
        def _(d):
            @pl.loop(0, 4)
            def _(j):
                i = k * 4 + j
                rows = pl.ds(pl.multiple_of(i * MSG, 8), MSG)

                @pl.when(i > 0)
                def _():
                    remote(
                        ob.at[d, rows, :], ret.at[d, rows, :], r_send, r_recv.at[d], peer(i, -1)
                    ).start()

                @pl.when(i == 0)
                def _():
                    pltpu.make_async_copy(ob.at[d, rows, :], ret.at[d, rows, :], r_own).start()

    @pl.loop(0, 4)
    def _(k):
        @pl.when(k < 2)
        def _():
            late_group(k + 2)

        @pl.when(k == 0)
        def _():
            wait_for(rb.at[:, pl.ds(0, 3 * MSG), :], d_recv.at[0])
            wait_for(rb.at[:, pl.ds(0, MSG), :], d_own)

        @pl.when(k > 0)
        def _():
            wait_for(rb.at[:, pl.ds(0, GR), :], d_recv.at[k])

        fetch(k)
        expert(k)
        send_back(k)

    wait_for(ret.at[:, pl.ds(0, MSG), :], r_own)

    @pl.loop(0, ND + 1)
    def _(t):
        @pl.when(t < ND)
        def _():
            d = jnp.minimum(t, ND - 1)
            wait_for(ret.at[d, pl.ds(0, ROWS - MSG), :], r_recv.at[d])
            cp = pltpu.make_async_copy(ret.at[d], retv, rv_sem)
            cp.start()
            cp.wait()
            for m in range(2):
                for n in range(3):
                    cols = slice(n * 256, (n + 1) * 256)
                    rows = pl.ds(pl.multiple_of(other + m * 256, 256), 256)
                    csb[d, m * 256 : (m + 1) * 256, cols] = dot(
                        place_t[rows, :], retv[:, cols]
                    ).astype(BF)
            remote(csb.at[d], crb.at[d], c_send, c_recv.at[d], sibling()).start()
            for m in range(2):
                for n in range(3):
                    cols = slice(n * 256, (n + 1) * 256)
                    here = slice(m * 256, (m + 1) * 256)
                    rows = pl.ds(pl.multiple_of(mine + m * 256, 256), 256)
                    wide = pl.ds(pl.multiple_of(d * CW + n * 256, 256), 256)
                    acc = dot(place_t[rows, :], retv[:, cols])
                    acc = acc + dot_last(sdg[here, :], sg[wide, :])
                    own[d, here, cols] = acc + dot_last(sdu[here, :], su[wide, :])

        @pl.when(t > 0)
        def _():
            d = jnp.maximum(t - 1, 0)
            wait_for(crb.at[d], c_recv.at[d])
            own[d] = own[d] + crb[d].astype(F32)
            for o in (2, 1, 3):
                slot = pl.ds(pl.multiple_of(((x + o) % 4) * TD, TD), TD)
                xsb[d, o - 1] = own[d, slot, :].astype(BF)
                remote(
                    xsb.at[d, o - 1], xrb.at[d, o - 1], x_send, x_recv.at[d], x_peer(o)
                ).start()

    @pl.loop(0, ND)
    def _(d):
        wait_for(xrb.at[d], x_recv.at[d])
        total = own[d, pl.ds(pl.multiple_of(x * TD, TD), TD), :]
        for o in range(3):
            total = total + xrb[d, o].astype(F32)
        fin[d] = total.astype(BF)

    for d in range(ND):
        pltpu.make_async_copy(fin.at[d], out.at[:, pl.ds(d * CW, CW)], f_sem).start()

    wait_for(meta_all.at[pl.ds(0, 7)], m_send)
    wait_for(xg.at[:, pl.ds(0, 3 * TD), :], gx_send)
    wait_for(xg.at[:, pl.ds(0, 4 * TD), :], gc_send)
    wait_for(sb.at[:, pl.ds(0, ROWS - MSG), :], d_send)
    wait_for(ob.at[:, pl.ds(0, ROWS - MSG), :], r_send)
    wait_for(csb, c_send)
    wait_for(xsb, x_send)
    wait_for(fin, f_sem)


def tables():
    r = np.arange(ROWS)
    i, b, s = r // MSG, (r // CAP) % NB, r % CAP
    expand = (np.arange(TD)[None, :] == (b * NPEER + i)[:, None]).astype(np.float32)
    slot_of = np.broadcast_to(s[:, None], (ROWS, TD)).astype(np.float32)
    block_of = np.broadcast_to(b[:, None], (ROWS, TD)).astype(np.float32)
    block_row = (b[None, :] == np.arange(NB)[:, None]).astype(np.float32)
    return expand, slot_of, block_of, block_row


def local(
    tokens,
    output_grad,
    chosen_experts,
    route_weights,
    gate_weight,
    up_weight,
    down_weight,
    gate_adapter_in,
    gate_adapter_out,
    up_adapter_in,
    up_adapter_out,
    shared_gate,
    shared_up,
    shared_down,
):
    z, y, c, x = position()
    g = jnp.arange(NB)[:, None]
    i = jnp.arange(NPEER)[None, :]
    zz = (z + i % 4 + i // 4) % 4
    yy = (y + i % 4) % 4
    ids = (((zz * 4 + yy) * 2 + g // 4) * 4 + g % 4).reshape(TD)
    same = chosen_experts.T[None, :, :] == ids[:, None, None]
    picked = jnp.any(same, axis=1)
    slot_weight = jnp.sum(jnp.where(same, route_weights.T[None, :, :], 0.0), axis=1)
    before = (jnp.arange(TD)[:, None] < jnp.arange(TD)[None, :]).astype(BF)
    place = jnp.dot(picked.astype(BF), before, preferred_element_type=F32)
    code = jnp.where(picked, place, -1.0)
    meta = jnp.stack(
        [code.reshape(NB, NPEER, TD), slot_weight.reshape(NB, NPEER, TD)], axis=1
    )
    expand, slot_of, block_of, block_row = tables()
    any_spec = pl.BlockSpec(memory_space=pl.ANY)
    vmem = pl.BlockSpec(memory_space=pltpu.VMEM)
    rank = gate_adapter_in.shape[1]
    sff = shared_gate.shape[1]
    dma = pltpu.SemaphoreType.DMA
    shape = jax.ShapeDtypeStruct
    outs = pl.pallas_call(
        kernel,
        name="moe_backward",
        out_shape=(
            shape((TD, D), BF),
            shape((rank, D), F32),
            shape((rank, FF), F32),
            shape((rank, D), F32),
            shape((rank, FF), F32),
            shape((NP, ROWS, CW), BF),
            shape((NP, ROWS, CW), BF),
            shape((ND, ROWS, CW), BF),
            shape((ND, ROWS, CW), BF),
        ),
        in_specs=[any_spec] * 3
        + [vmem] * 4
        + [any_spec] * 3
        + [vmem] * 4
        + [any_spec] * 3,
        out_specs=(any_spec, vmem, vmem, vmem, vmem) + (any_spec,) * 4,
        scratch_shapes=[
            pltpu.VMEM((D, FF), BF),
            pltpu.VMEM((D, FF), BF),
            pltpu.VMEM((FF, D), BF),
            pltpu.VMEM((D, sff), BF),
            pltpu.VMEM((D, sff), BF),
            pltpu.VMEM((D, sff), BF),
            pltpu.VMEM((NB, 2, NPEER, TD), F32),
            pltpu.VMEM((NP, NB * TD, CW), BF),
            pltpu.VMEM((ROWS, NB * TD), BF),
            pltpu.VMEM((NB * TD, ROWS), BF),
            pltpu.VMEM((ROWS, TD), F32),
            pltpu.VMEM((2, GR, CW), F32),
            pltpu.VMEM((2, GR, CW), BF),
            pltpu.VMEM((ND, GR, CW), BF),
            pltpu.VMEM((ND, GR, CW), BF),
            pltpu.VMEM((GR, FF), BF),
            pltpu.VMEM((GR, FF), BF),
            pltpu.VMEM((ND, GR, CW), BF),
            pltpu.VMEM((HALF, sff), F32),
            pltpu.VMEM((HALF, sff), F32),
            pltpu.VMEM((HALF, sff), F32),
            pltpu.VMEM((HALF, sff), BF),
            pltpu.VMEM((HALF, sff), BF),
            pltpu.VMEM((ROWS, CW), BF),
            pltpu.VMEM((ND, HALF, CW), F32),
            pltpu.VMEM((ND, HALF, CW), BF),
            pltpu.VMEM((ND, HALF, CW), BF),
            pltpu.VMEM((ND, 3, TD, CW), BF),
            pltpu.VMEM((ND, 3, TD, CW), BF),
            pltpu.VMEM((ND, TD, CW), BF),
            dma((3,)),
            dma,
            dma,
            dma,
            dma,
            dma((NP,)),
            dma,
            dma((NP, 3)),
            dma,
            dma((NP,)),
            dma,
            dma,
            dma((4,)),
            dma,
            dma,
            dma,
            dma,
            dma((ND,)),
            dma,
            dma,
            dma,
            dma((ND,)),
            dma,
            dma((ND,)),
            dma,
        ],
        compiler_params=pltpu.CompilerParams(
            collective_id=0, has_side_effects=True, vmem_limit_bytes=62 << 20
        ),
    )(
        tokens,
        output_grad,
        meta,
        jnp.asarray(expand, BF),
        jnp.asarray(slot_of),
        jnp.asarray(block_of),
        jnp.asarray(block_row),
        gate_weight[0],
        up_weight[0],
        down_weight[0],
        gate_adapter_in[0],
        gate_adapter_out[0],
        up_adapter_in[0],
        up_adapter_out[0],
        shared_gate,
        shared_up,
        shared_down,
    )
    return (outs[0], outs[1][None], outs[2][None], outs[3][None], outs[4][None])


def solution(mesh):
    in_specs = (
        (P(("ep", "rep"), None),) * 4 + (P(("ep", "rep"), None, None),) * 7 + (P(None, "rep"),) * 3
    )
    out_specs = (P(("ep", "rep"), None),) + (P(("ep", "rep"), None, None),) * 4
    return jax.shard_map(
        local, mesh=mesh, in_specs=in_specs, out_specs=out_specs, check_vma=False
    )
```

```python
import functools

import jax
import jax.numpy as jnp
import numpy as np
from jax import lax
from jax.experimental import pallas as pl
from jax.experimental.pallas import tpu as pltpu
from jax.sharding import PartitionSpec as P

MESH = pl.DeviceIdType.MESH
BF = jnp.bfloat16
F32 = jnp.float32

TD = 128
D = 2304
FF = 1024
CAP = 9
NB = 8
NPEER = 16
MSG = NB * CAP
ROWS = NPEER * MSG
GR = 4 * MSG
ND = 3
CW = D // ND
NP = 2 * ND
HALF = 4 * TD


def dot(a, b):
    return jnp.dot(a, b, preferred_element_type=F32)


def dot_last(a, b):
    return lax.dot_general(a, b, (((1,), (1,)), ((), ())), preferred_element_type=F32)


def dot_first(a, b):
    return lax.dot_general(a, b, (((0,), (0,)), ((), ())), preferred_element_type=F32)


def position():
    e, x = lax.axis_index("ep"), lax.axis_index("rep")
    return e // 8, (e // 2) % 4, e % 2, x


def peer(i, sign):
    z, y, c, x = position()
    oy = i % 4
    oz = (i % 4 + i // 4) % 4
    zz = (z + sign * oz + 4) % 4
    yy = (y + sign * oy + 4) % 4
    return {"ep": (zz * 4 + yy) * 2 + c, "rep": x}


def x_peer(o):
    z, y, c, x = position()
    return {"ep": (z * 4 + y) * 2 + c, "rep": (x + o) % 4}


def member(o):
    z, y, c, x = position()
    return {"ep": (z * 4 + y) * 2 + (c + o // 4) % 2, "rep": (x + o) % 4}


def member_slot(o):
    z, y, c, x = position()
    return ((c + o // 4) % 2) * 4 + (x + o) % 4


def sibling():
    z, y, c, x = position()
    return {"ep": (z * 4 + y) * 2 + 1 - c, "rep": x}


def remote(src, dst, send, recv, device):
    return pltpu.make_async_remote_copy(
        src_ref=src,
        dst_ref=dst,
        send_sem=send,
        recv_sem=recv,
        device_id=device,
        device_id_type=MESH,
    )


def wait_for(ref, sem):
    pltpu.make_async_copy(ref, ref, sem).wait()


def kernel(
    tok,
    grd,
    chosen,
    route,
    expand,
    slot_of,
    block_of,
    block_row,
    gw_h,
    uw_h,
    dw_h,
    gin,
    gout,
    uin,
    uout,
    sg_h,
    su_h,
    sd_h,
    out,
    gin_g,
    gout_g,
    uin_g,
    uout_g,
    sb,
    rb,
    ob,
    ret,
    gw,
    uw,
    dw,
    sg,
    su,
    sd,
    meta,
    meta_all,
    xg,
    place,
    place_t,
    wsl,
    tmp,
    stage,
    xb,
    gb,
    dg,
    du,
    outb,
    kept,
    sga,
    sua,
    sda,
    sdg,
    sdu,
    retv,
    own,
    csb,
    crb,
    xsb,
    xrb,
    fin,
    w_sem,
    s_sem,
    m_send,
    m_recv,
    m_own,
    own_sem,
    gx_send,
    gx_recv,
    gc_send,
    gc_recv,
    st_sem,
    d_send,
    d_recv,
    d_own,
    in_sem,
    o_sem,
    r_send,
    r_recv,
    r_own,
    rv_sem,
    c_send,
    c_recv,
    x_send,
    x_recv,
    f_sem,
):
    z, y, c, x = position()
    me = c * 4 + x

    barrier = pltpu.get_barrier_semaphore()

    @pl.loop(1, NPEER)
    def _(i):
        pl.semaphore_signal(barrier, inc=1, device_id=peer(i, 1), device_id_type=MESH)

    @pl.loop(1, 8)
    def _(o):
        pl.semaphore_signal(barrier, inc=1, device_id=member(o), device_id_type=MESH)

    weights = [(gw_h, gw), (uw_h, uw), (dw_h, dw)]
    shared = [(sg_h, sg), (su_h, su), (sd_h, sd)]

    def own_piece(p):
        src = tok if p < ND else grd
        return pltpu.make_async_copy(
            src.at[:, pl.ds((p % ND) * CW, CW)],
            xg.at[p, pl.ds(me * TD, TD), :],
            own_sem.at[p],
        )

    for p in range(NP):
        own_piece(p).start()
    for h, v in shared:
        pltpu.make_async_copy(h, v, s_sem).start()
    for j, (h, v) in enumerate(weights):
        pltpu.make_async_copy(h, v, w_sem.at[j]).start()
    gin_g[...] = jnp.zeros_like(gin_g)
    gout_g[...] = jnp.zeros_like(gout_g)
    uin_g[...] = jnp.zeros_like(uin_g)
    uout_g[...] = jnp.zeros_like(uout_g)
    sga[...] = jnp.zeros_like(sga)
    sua[...] = jnp.zeros_like(sua)
    sda[...] = jnp.zeros_like(sda)

    row_i = lax.broadcasted_iota(jnp.int32, (TD, TD), 0)
    col_i = lax.broadcasted_iota(jnp.int32, (TD, TD), 1)
    group, chip = row_i >> 4, row_i & 15
    zz = (z + (chip & 3) + (chip >> 2)) & 3
    yy = (y + (chip & 3)) & 3
    ids = (((zz * 4 + yy) * 2 + (group >> 2)) * 4) + (group & 3)
    picked = jnp.zeros((TD, TD), F32)
    weight = jnp.zeros((TD, TD), F32)
    for k in range(chosen.shape[0]):
        same = chosen[k : k + 1, :] == ids
        picked = jnp.where(same, 1.0, picked)
        weight = jnp.where(same, route[k : k + 1, :], weight)
    before = jnp.where(row_i < col_i, 1.0, 0.0).astype(BF)
    count = dot(picked.astype(BF), before)
    meta[:, 0] = jnp.where(picked > 0.0, count, -1.0).reshape(NB, NPEER, TD)
    meta[:, 1] = weight.reshape(NB, NPEER, TD)
    own_meta = pltpu.make_async_copy(meta.at[me], meta_all.at[me], m_own)
    own_meta.start()

    pl.semaphore_wait(barrier, NPEER - 1 + 7)

    @pl.loop(1, 8)
    def _(o):
        remote(meta.at[member_slot(o)], meta_all.at[me], m_send, m_recv, member(o)).start()

    for p in range(NP):
        src = (tok if p < ND else grd).at[:, pl.ds((p % ND) * CW, CW)]
        dst = xg.at[p, pl.ds(me * TD, TD), :]
        for o in (1, 3, 2):
            remote(src, dst, gx_send, gx_recv.at[p, o - 1], x_peer(o)).start()
        remote(src, dst, gc_send, gc_recv.at[p], sibling()).start()

    own_meta.wait()
    wait_for(meta_all.at[pl.ds(0, 7)], m_recv)

    spread = expand[...]
    code = meta_all[:, 0].reshape(TD, TD).astype(BF)
    hit = jnp.where(dot(spread, code) == slot_of[...], 1.0, 0.0)
    w_all = meta_all[:, 1].reshape(TD, TD)
    w_hi = w_all.astype(BF)
    left = w_all - w_hi.astype(F32)
    w_mid = left.astype(BF)
    w_lo = (left - w_mid.astype(F32)).astype(BF)
    w_row = (dot(spread, w_hi) + dot(spread, w_mid)) + dot(spread, w_lo)
    wsl[...] = jnp.broadcast_to(jnp.sum(w_row * hit, axis=1, keepdims=True), (ROWS, TD))
    hit_t = hit.T
    for b in range(NB):
        place[:, b * TD : (b + 1) * TD] = jnp.where(block_of[...] == float(b), hit, 0.0).astype(BF)
        place_t[b * TD : (b + 1) * TD, :] = (hit_t * block_row[b : b + 1, :]).astype(BF)

    wait_shared = [pltpu.make_async_copy(h, v, s_sem) for h, v in shared]
    for cp in wait_shared:
        cp.wait()

    mine = pl.multiple_of(c * HALF, HALF)
    other = pl.multiple_of((1 - c) * HALF, HALF)

    def rows_of(k):
        return pl.ds(pl.multiple_of(k * GR, 8), GR)

    def send_piece(p, k, slot):
        cp = pltpu.make_async_copy(stage.at[slot], sb.at[p, rows_of(k), :], st_sem)
        cp.start()
        cp.wait()

        @pl.loop(0, 4)
        def _(j):
            i = k * 4 + j
            rows = pl.ds(pl.multiple_of(i * MSG, 8), MSG)

            @pl.when(i > 0)
            def _():
                remote(
                    sb.at[p, rows, :], rb.at[p, rows, :], d_send, d_recv.at[k], peer(i, 1)
                ).start()

            @pl.when(i == 0)
            def _():
                kept[p] = stage[slot, 0:MSG, :]
                pltpu.make_async_copy(kept.at[p], rb.at[p, rows, :], d_own).start()

    def scaled(acc, p, k):
        scale = jnp.where(p < ND, 1.0, wsl[rows_of(k), :][:, 0:1])
        return (acc * scale).astype(BF)

    def arrive(p):
        for o in (1, 3, 2):
            slot = pl.ds(pl.multiple_of((c * 4 + (x + 4 - o) % 4) * TD, TD), TD)
            block = xg.at[p, slot, :]
            wait_for(block, gx_recv.at[p, o - 1])
            remote(block, block, gc_send, gc_recv.at[p], sibling()).start()

    def first_groups(p, shared_part):
        arrive(p)

        @pl.loop(0, 2)
        def _(k):
            for n in range(3):
                cols = slice(n * 256, (n + 1) * 256)
                tmp[k, :, cols] = dot(
                    place[rows_of(k), pl.ds(mine, HALF)], xg[p, pl.ds(mine, HALF), cols]
                )

        wait_for(xg.at[p, pl.ds(other, HALF), :], gc_recv.at[p])

        @pl.loop(0, 2)
        def _(k):
            for n in range(3):
                cols = slice(n * 256, (n + 1) * 256)
                acc = tmp[k, :, cols] + dot(
                    place[rows_of(k), pl.ds(other, HALF)], xg[p, pl.ds(other, HALF), cols]
                )
                stage[k, :, cols] = scaled(acc, p, k)
            send_piece(p, k, k)

        shared_part(xg[p, pl.ds(mine, HALF), :])

    @pl.loop(0, ND)
    def _(d):
        pltpu.make_async_copy(
            tok.at[:, pl.ds(0, CW)], xg.at[d, pl.ds(me * TD, TD), :], own_sem.at[d]
        ).wait()
        rows = pl.ds(pl.multiple_of(d * CW, CW), CW)

        def part(block):
            sga[...] += dot(block, sg[rows, :])
            sua[...] += dot(block, su[rows, :])

        first_groups(d, part)

    @pl.loop(0, ND)
    def _(d):
        p = d + ND
        pltpu.make_async_copy(
            tok.at[:, pl.ds(0, CW)], xg.at[p, pl.ds(me * TD, TD), :], own_sem.at[p]
        ).wait()
        rows = pl.ds(pl.multiple_of(d * CW, CW), CW)

        def part(block):
            sda[...] += dot(block, sd[rows, :])

        first_groups(p, part)

    s_gate, s_up, s_hid = sga[...], sua[...], sda[...]
    sig = jax.nn.sigmoid(s_gate)
    sdg[...] = (s_hid * s_up * sig * (1.0 + s_gate * (1.0 - sig))).astype(BF)
    sdu[...] = (s_hid * s_gate * sig).astype(BF)

    for j, (h, v) in enumerate(weights):
        pltpu.make_async_copy(h, v, w_sem.at[j]).wait()

    def late_piece(k, p):
        for n in range(3):
            cols = slice(n * 256, (n + 1) * 256)
            acc = dot(place[rows_of(k), :], xg[p, :, cols])
            stage[0, :, cols] = scaled(acc, p, k)
        send_piece(p, k, 0)

    def fetch(k):
        for d in range(ND):
            pltpu.make_async_copy(rb.at[d, rows_of(k), :], xb.at[d], in_sem).start()
            pltpu.make_async_copy(rb.at[ND + d, rows_of(k), :], gb.at[d], in_sem).start()
        wait_for(xb, in_sem)
        wait_for(gb, in_sem)

    def expert(k):
        low_gate = sum(dot_last(xb[d], gin[:, d * CW : (d + 1) * CW]) for d in range(ND)).astype(BF)
        low_up = sum(dot_last(xb[d], uin[:, d * CW : (d + 1) * CW]) for d in range(ND)).astype(BF)

        @pl.loop(0, FF // 256)
        def _(j):
            cols = pl.ds(pl.multiple_of(j * 256, 256), 256)
            gate = sum(dot(xb[d], gw[d * CW : (d + 1) * CW, cols]) for d in range(ND))
            gate = gate + dot(low_gate, gout[:, cols])
            up = sum(dot(xb[d], uw[d * CW : (d + 1) * CW, cols]) for d in range(ND))
            up = up + dot(low_up, uout[:, cols])
            hid = sum(dot_last(gb[d], dw[cols, d * CW : (d + 1) * CW]) for d in range(ND))
            s = jax.nn.sigmoid(gate)
            dg[:, cols] = (hid * up * s * (1.0 + gate * (1.0 - s))).astype(BF)
            du[:, cols] = (hid * gate * s).astype(BF)

        dgv, duv = dg[...], du[...]
        low_dg = dot_last(dgv, gout[...]).astype(BF)
        low_du = dot_last(duv, uout[...]).astype(BF)
        gout_g[...] += dot_first(low_gate, dgv)
        uout_g[...] += dot_first(low_up, duv)
        for d in range(ND):
            cols = slice(d * CW, (d + 1) * CW)
            gin_g[:, cols] += dot_first(low_dg, xb[d])
            uin_g[:, cols] += dot_first(low_du, xb[d])

        @pl.loop(0, ND)
        def _(d):
            for n in range(3):
                rows = pl.ds(pl.multiple_of(d * CW + n * 256, 256), 256)
                acc = dot_last(dg[...], gw[rows, :]) + dot(low_dg, gin[:, rows])
                acc = acc + dot_last(du[...], uw[rows, :]) + dot(low_du, uin[:, rows])
                outb[d, :, n * 256 : (n + 1) * 256] = acc.astype(BF)

    def store(k):
        for d in range(ND):
            pltpu.make_async_copy(outb.at[d], ob.at[d, rows_of(k), :], o_sem).start()
        wait_for(outb, o_sem)

        @pl.when(k == 0)
        def _():
            for d in range(ND):
                kept[d] = outb[d, 0:MSG, :]
                pltpu.make_async_copy(kept.at[d], ret.at[d, pl.ds(0, MSG), :], r_own).start()

    def send_back(k_from, k_to, d_from, d_to):
        @pl.loop(d_from, d_to)
        def _(d):
            @pl.loop(4 * k_from, 4 * k_to)
            def _(i):
                rows = pl.ds(pl.multiple_of(i * MSG, 8), MSG)

                @pl.when(i > 0)
                def _():
                    remote(
                        ob.at[d, rows, :], ret.at[d, rows, :], r_send, r_recv.at[d], peer(i, -1)
                    ).start()


    @pl.loop(2, 4)
    def _(k):
        @pl.loop(0, NP)
        def _(p):
            late_piece(k, p)

    @pl.loop(0, 4)
    def _(k):
        @pl.when(k == 0)
        def _():
            wait_for(rb.at[:, pl.ds(0, 3 * MSG), :], d_recv.at[0])
            wait_for(rb.at[:, pl.ds(0, MSG), :], d_own)

        @pl.when(k > 0)
        def _():
            wait_for(rb.at[:, pl.ds(0, GR), :], d_recv.at[k])

        fetch(k)
        expert(k)
        store(k)

        @pl.when(k < 3)
        def _():
            send_back(k, k + 1, 0, 1)

        @pl.when(k == 2)
        def _():
            send_back(0, 3, 1, 2)

        @pl.when(k == 3)
        def _():
            send_back(3, 4, 0, 2)
            send_back(0, 4, 2, 3)

    wait_for(ret.at[:, pl.ds(0, MSG), :], r_own)

    @pl.loop(0, ND + 1)
    def _(t):
        @pl.when(t < ND)
        def _():
            d = jnp.minimum(t, ND - 1)
            wait_for(ret.at[d, pl.ds(0, ROWS - MSG), :], r_recv.at[d])
            cp = pltpu.make_async_copy(ret.at[d], retv, rv_sem)
            cp.start()
            cp.wait()
            for m in range(2):
                for n in range(3):
                    cols = slice(n * 256, (n + 1) * 256)
                    rows = pl.ds(pl.multiple_of(other + m * 256, 256), 256)
                    csb[d, m * 256 : (m + 1) * 256, cols] = dot(
                        place_t[rows, :], retv[:, cols]
                    ).astype(BF)
            remote(csb.at[d], crb.at[d], c_send, c_recv.at[d], sibling()).start()
            for m in range(2):
                for n in range(3):
                    cols = slice(n * 256, (n + 1) * 256)
                    here = slice(m * 256, (m + 1) * 256)
                    rows = pl.ds(pl.multiple_of(mine + m * 256, 256), 256)
                    wide = pl.ds(pl.multiple_of(d * CW + n * 256, 256), 256)
                    acc = dot(place_t[rows, :], retv[:, cols])
                    acc = acc + dot_last(sdg[here, :], sg[wide, :])
                    own[d, here, cols] = acc + dot_last(sdu[here, :], su[wide, :])

        @pl.when(t > 0)
        def _():
            d = jnp.maximum(t - 1, 0)
            wait_for(crb.at[d], c_recv.at[d])
            own[d] = own[d] + crb[d].astype(F32)
            for o in (2, 1, 3):
                slot = pl.ds(pl.multiple_of(((x + o) % 4) * TD, TD), TD)
                xsb[d, o - 1] = own[d, slot, :].astype(BF)
                remote(
                    xsb.at[d, o - 1], xrb.at[d, o - 1], x_send, x_recv.at[d], x_peer(o)
                ).start()

    @pl.loop(0, ND)
    def _(d):
        wait_for(xrb.at[d], x_recv.at[d])
        total = own[d, pl.ds(pl.multiple_of(x * TD, TD), TD), :]
        for o in range(3):
            total = total + xrb[d, o].astype(F32)
        fin[d] = total.astype(BF)

    for d in range(ND):
        pltpu.make_async_copy(fin.at[d], out.at[:, pl.ds(d * CW, CW)], f_sem).start()

    wait_for(meta_all.at[pl.ds(0, 7)], m_send)
    wait_for(xg.at[:, pl.ds(0, 3 * TD), :], gx_send)
    wait_for(xg.at[:, pl.ds(0, 4 * TD), :], gc_send)
    wait_for(sb.at[:, pl.ds(0, ROWS - MSG), :], d_send)
    wait_for(ob.at[:, pl.ds(0, ROWS - MSG), :], r_send)
    wait_for(csb, c_send)
    wait_for(xsb, x_send)
    wait_for(fin, f_sem)


def hand_over(*refs):
    for j in range(5):
        refs[5 + j][...] = refs[j][...].reshape(refs[5 + j].shape)


def tables():
    r = np.arange(ROWS)
    i, b, s = r // MSG, (r // CAP) % NB, r % CAP
    expand = (np.arange(TD)[None, :] == (b * NPEER + i)[:, None]).astype(np.float32)
    slot_of = np.broadcast_to(s[:, None], (ROWS, TD)).astype(np.float32)
    block_of = np.broadcast_to(b[:, None], (ROWS, TD)).astype(np.float32)
    block_row = (b[None, :] == np.arange(NB)[:, None]).astype(np.float32)
    return expand, slot_of, block_of, block_row


def local(
    tokens,
    output_grad,
    chosen_experts,
    route_weights,
    gate_weight,
    up_weight,
    down_weight,
    gate_adapter_in,
    gate_adapter_out,
    up_adapter_in,
    up_adapter_out,
    shared_gate,
    shared_up,
    shared_down,
):
    expand, slot_of, block_of, block_row = tables()
    any_spec = pl.BlockSpec(memory_space=pl.ANY)
    vmem = pl.BlockSpec(memory_space=pltpu.VMEM)
    rank = gate_adapter_in.shape[1]
    sff = shared_gate.shape[1]
    dma = pltpu.SemaphoreType.DMA
    shape = jax.ShapeDtypeStruct
    outs = pl.pallas_call(
        kernel,
        name="moe_backward",
        out_shape=(
            shape((TD, D), BF),
            shape((rank, D), F32),
            shape((rank, FF), F32),
            shape((rank, D), F32),
            shape((rank, FF), F32),
            shape((NP, ROWS, CW), BF),
            shape((NP, ROWS, CW), BF),
            shape((ND, ROWS, CW), BF),
            shape((ND, ROWS, CW), BF),
        ),
        in_specs=[any_spec] * 2
        + [vmem] * 6
        + [any_spec] * 3
        + [vmem] * 4
        + [any_spec] * 3,
        out_specs=(any_spec, vmem, vmem, vmem, vmem) + (any_spec,) * 4,
        scratch_shapes=[
            pltpu.VMEM((D, FF), BF),
            pltpu.VMEM((D, FF), BF),
            pltpu.VMEM((FF, D), BF),
            pltpu.VMEM((D, sff), BF),
            pltpu.VMEM((D, sff), BF),
            pltpu.VMEM((D, sff), BF),
            pltpu.VMEM((NB, 2, NPEER, TD), F32),
            pltpu.VMEM((NB, 2, NPEER, TD), F32),
            pltpu.VMEM((NP, NB * TD, CW), BF),
            pltpu.VMEM((ROWS, NB * TD), BF),
            pltpu.VMEM((NB * TD, ROWS), BF),
            pltpu.VMEM((ROWS, TD), F32),
            pltpu.VMEM((2, GR, CW), F32),
            pltpu.VMEM((2, GR, CW), BF),
            pltpu.VMEM((ND, GR, CW), BF),
            pltpu.VMEM((ND, GR, CW), BF),
            pltpu.VMEM((GR, FF), BF),
            pltpu.VMEM((GR, FF), BF),
            pltpu.VMEM((ND, GR, CW), BF),
            pltpu.VMEM((NP, MSG, CW), BF),
            pltpu.VMEM((HALF, sff), F32),
            pltpu.VMEM((HALF, sff), F32),
            pltpu.VMEM((HALF, sff), F32),
            pltpu.VMEM((HALF, sff), BF),
            pltpu.VMEM((HALF, sff), BF),
            pltpu.VMEM((ROWS, CW), BF),
            pltpu.VMEM((ND, HALF, CW), F32),
            pltpu.VMEM((ND, HALF, CW), BF),
            pltpu.VMEM((ND, HALF, CW), BF),
            pltpu.VMEM((ND, 3, TD, CW), BF),
            pltpu.VMEM((ND, 3, TD, CW), BF),
            pltpu.VMEM((ND, TD, CW), BF),
            dma((3,)),
            dma,
            dma,
            dma,
            dma,
            dma((NP,)),
            dma,
            dma((NP, 3)),
            dma,
            dma((NP,)),
            dma,
            dma,
            dma((4,)),
            dma,
            dma,
            dma,
            dma,
            dma((ND,)),
            dma,
            dma,
            dma,
            dma((ND,)),
            dma,
            dma((ND,)),
            dma,
        ],
        compiler_params=pltpu.CompilerParams(
            collective_id=0, has_side_effects=True, vmem_limit_bytes=62 << 20
        ),
    )(
        tokens,
        output_grad,
        chosen_experts.T,
        route_weights.T,
        jnp.asarray(expand, BF),
        jnp.asarray(slot_of),
        jnp.asarray(block_of),
        jnp.asarray(block_row),
        gate_weight[0],
        up_weight[0],
        down_weight[0],
        gate_adapter_in[0],
        gate_adapter_out[0],
        up_adapter_in[0],
        up_adapter_out[0],
        shared_gate,
        shared_up,
        shared_down,
    )
    return pl.pallas_call(
        hand_over,
        name="hand_over",
        out_shape=(
            shape((TD, D), BF),
            shape((1, rank, D), F32),
            shape((1, rank, FF), F32),
            shape((1, rank, D), F32),
            shape((1, rank, FF), F32),
        ),
        in_specs=[vmem] * 5,
        out_specs=(vmem,) * 5,
    )(*outs[:5])


def solution(mesh):
    in_specs = (
        (P(("ep", "rep"), None),) * 4 + (P(("ep", "rep"), None, None),) * 7 + (P(None, "rep"),) * 3
    )
    out_specs = (P(("ep", "rep"), None),) + (P(("ep", "rep"), None, None),) * 4
    return jax.shard_map(
        local, mesh=mesh, in_specs=in_specs, out_specs=out_specs, check_vma=False
    )
```

```python
import functools

import jax
import jax.numpy as jnp
import numpy as np
from jax import lax
from jax.experimental import pallas as pl
from jax.experimental.pallas import tpu as pltpu
from jax.sharding import PartitionSpec as P

MESH = pl.DeviceIdType.MESH
BF = jnp.bfloat16
F32 = jnp.float32

TD = 128
D = 2304
FF = 1024
CAP = 9
NB = 8
NPEER = 16
MSG = NB * CAP
ROWS = NPEER * MSG
GR = 4 * MSG
ND = 3
CW = D // ND
NP = 2 * ND
HALF = 4 * TD
UW = 256
NU = D // UW
FIRST = 3


def dot(a, b):
    return jnp.dot(a, b, preferred_element_type=F32)


def dot_last(a, b):
    return lax.dot_general(a, b, (((1,), (1,)), ((), ())), preferred_element_type=F32)


def dot_first(a, b):
    return lax.dot_general(a, b, (((0,), (0,)), ((), ())), preferred_element_type=F32)


def position():
    e, x = lax.axis_index("ep"), lax.axis_index("rep")
    return e // 8, (e // 2) % 4, e % 2, x


def peer(i, sign):
    z, y, c, x = position()
    oy = i % 4
    oz = (i % 4 + i // 4) % 4
    zz = (z + sign * oz + 4) % 4
    yy = (y + sign * oy + 4) % 4
    return {"ep": (zz * 4 + yy) * 2 + c, "rep": x}


def x_peer(o):
    z, y, c, x = position()
    return {"ep": (z * 4 + y) * 2 + c, "rep": (x + o) % 4}


def member(o):
    z, y, c, x = position()
    return {"ep": (z * 4 + y) * 2 + (c + o // 4) % 2, "rep": (x + o) % 4}


def member_slot(o):
    z, y, c, x = position()
    return ((c + o // 4) % 2) * 4 + (x + o) % 4


def sibling():
    z, y, c, x = position()
    return {"ep": (z * 4 + y) * 2 + 1 - c, "rep": x}


def remote(src, dst, send, recv, device):
    return pltpu.make_async_remote_copy(
        src_ref=src,
        dst_ref=dst,
        send_sem=send,
        recv_sem=recv,
        device_id=device,
        device_id_type=MESH,
    )


def wait_for(ref, sem):
    pltpu.make_async_copy(ref, ref, sem).wait()


def kernel(
    tok,
    grd,
    chosen,
    route,
    expand,
    slot_of,
    block_of,
    block_row,
    gw_h,
    uw_h,
    dw_h,
    gin,
    gout,
    uin,
    uout,
    sg_h,
    su_h,
    sd_h,
    out,
    gin_g,
    gout_g,
    uin_g,
    uout_g,
    sb,
    rb,
    ob,
    ret,
    gw,
    uw,
    dw,
    sg,
    su,
    sd,
    meta,
    meta_all,
    xg,
    place,
    place_t,
    wsl,
    hits,
    tmp,
    stage,
    xb,
    gb,
    dg,
    du,
    outb,
    kept,
    back,
    sga,
    sua,
    sda,
    sdg,
    sdu,
    retv,
    own,
    csb,
    crb,
    xsb,
    xrb,
    fin,
    w_sem,
    s_sem,
    m_send,
    m_recv,
    m_own,
    own_sem,
    gx_send,
    gx_recv,
    gc_send,
    gc_recv,
    st_sem,
    d_send,
    d_recv,
    d_own,
    in_sem,
    o_sem,
    r_send,
    r_recv,
    r_own,
    rv_sem,
    c_send,
    c_recv,
    x_send,
    x_recv,
    f_sem,
):
    z, y, c, x = position()
    me = c * 4 + x

    barrier = pltpu.get_barrier_semaphore()

    @pl.loop(1, NPEER)
    def _(i):
        pl.semaphore_signal(barrier, inc=1, device_id=peer(i, 1), device_id_type=MESH)

    @pl.loop(1, 8)
    def _(o):
        pl.semaphore_signal(barrier, inc=1, device_id=member(o), device_id_type=MESH)

    weights = [(gw_h, gw), (uw_h, uw), (dw_h, dw)]
    shared = [(sg_h, sg), (su_h, su), (sd_h, sd)]

    def own_piece(p):
        src = tok if p < ND else grd
        return pltpu.make_async_copy(
            src.at[:, pl.ds((p % ND) * CW, CW)],
            xg.at[p, pl.ds(me * TD, TD), :],
            own_sem.at[p],
        )

    for p in range(NP):
        own_piece(p).start()
    for h, v in shared:
        pltpu.make_async_copy(h, v, s_sem).start()
    for j, (h, v) in enumerate(weights):
        pltpu.make_async_copy(h, v, w_sem.at[j]).start()
    gin_g[...] = jnp.zeros_like(gin_g)
    gout_g[...] = jnp.zeros_like(gout_g)
    uin_g[...] = jnp.zeros_like(uin_g)
    uout_g[...] = jnp.zeros_like(uout_g)
    sga[...] = jnp.zeros_like(sga)
    sua[...] = jnp.zeros_like(sua)
    sda[...] = jnp.zeros_like(sda)

    row_i = lax.broadcasted_iota(jnp.int32, (TD, TD), 0)
    col_i = lax.broadcasted_iota(jnp.int32, (TD, TD), 1)
    group, chip = row_i >> 4, row_i & 15
    zz = (z + (chip & 3) + (chip >> 2)) & 3
    yy = (y + (chip & 3)) & 3
    ids = (((zz * 4 + yy) * 2 + (group >> 2)) * 4) + (group & 3)
    picked = jnp.zeros((TD, TD), F32)
    weight = jnp.zeros((TD, TD), F32)
    for k in range(chosen.shape[0]):
        same = chosen[k : k + 1, :] == ids
        picked = jnp.where(same, 1.0, picked)
        weight = jnp.where(same, route[k : k + 1, :], weight)
    before = jnp.where(row_i < col_i, 1.0, 0.0).astype(BF)
    count = dot(picked.astype(BF), before)
    meta[:, 0] = jnp.where(picked > 0.0, count, -1.0).reshape(NB, NPEER, TD)
    meta[:, 1] = weight.reshape(NB, NPEER, TD)
    own_meta = pltpu.make_async_copy(meta.at[me], meta_all.at[me], m_own)
    own_meta.start()

    pl.semaphore_wait(barrier, NPEER - 1 + 7)

    @pl.loop(1, 8)
    def _(o):
        remote(meta.at[member_slot(o)], meta_all.at[me], m_send, m_recv, member(o)).start()

    for p in range(NP):
        src = (tok if p < ND else grd).at[:, pl.ds((p % ND) * CW, CW)]
        dst = xg.at[p, pl.ds(me * TD, TD), :]
        for o in (1, 3, 2):
            remote(src, dst, gx_send, gx_recv.at[p, o - 1], x_peer(o)).start()
        remote(src, dst, gc_send, gc_recv.at[p], sibling()).start()

    own_meta.wait()
    wait_for(meta_all.at[pl.ds(0, 7)], m_recv)

    spread = expand[...]
    code = meta_all[:, 0].reshape(TD, TD).astype(BF)
    hit = jnp.where(dot(spread, code) == slot_of[...], 1.0, 0.0)
    w_all = meta_all[:, 1].reshape(TD, TD)
    w_hi = w_all.astype(BF)
    left = w_all - w_hi.astype(F32)
    w_mid = left.astype(BF)
    w_lo = (left - w_mid.astype(F32)).astype(BF)
    w_row = (dot(spread, w_hi) + dot(spread, w_mid)) + dot(spread, w_lo)
    wsl[...] = jnp.broadcast_to(jnp.sum(w_row * hit, axis=1, keepdims=True), (ROWS, TD))
    hits[...] = hit
    for b in range(NB):
        place[:, b * TD : (b + 1) * TD] = jnp.where(block_of[...] == float(b), hit, 0.0).astype(BF)

    wait_shared = [pltpu.make_async_copy(h, v, s_sem) for h, v in shared]
    for cp in wait_shared:
        cp.wait()

    mine = pl.multiple_of(c * HALF, HALF)
    other = pl.multiple_of((1 - c) * HALF, HALF)

    def rows_of(k):
        return pl.ds(pl.multiple_of(k * GR, 8), GR)

    def send_piece(p, k, slot):
        cp = pltpu.make_async_copy(stage.at[slot], sb.at[p, rows_of(k), :], st_sem)
        cp.start()
        cp.wait()

        @pl.loop(0, 4)
        def _(j):
            i = k * 4 + j
            rows = pl.ds(pl.multiple_of(i * MSG, 8), MSG)

            @pl.when(i > 0)
            def _():
                remote(
                    sb.at[p, rows, :], rb.at[p, rows, :], d_send, d_recv.at[k], peer(i, 1)
                ).start()

            @pl.when(i == 0)
            def _():
                kept[p] = stage[slot, 0:MSG, :]
                pltpu.make_async_copy(kept.at[p], rb.at[p, rows, :], d_own).start()

    def scaled(acc, p, k):
        scale = jnp.where(p < ND, 1.0, wsl[rows_of(k), :][:, 0:1])
        return (acc * scale).astype(BF)

    def arrive(p):
        for o in (1, 3, 2):
            slot = pl.ds(pl.multiple_of((c * 4 + (x + 4 - o) % 4) * TD, TD), TD)
            block = xg.at[p, slot, :]
            wait_for(block, gx_recv.at[p, o - 1])
            remote(block, block, gc_send, gc_recv.at[p], sibling()).start()

    def first_groups(p, shared_part):
        arrive(p)

        @pl.loop(0, FIRST)
        def _(k):
            for n in range(3):
                cols = slice(n * 256, (n + 1) * 256)
                tmp[k, :, cols] = dot(
                    place[rows_of(k), pl.ds(mine, HALF)], xg[p, pl.ds(mine, HALF), cols]
                )

        wait_for(xg.at[p, pl.ds(other, HALF), :], gc_recv.at[p])

        @pl.loop(0, FIRST)
        def _(k):
            for n in range(3):
                cols = slice(n * 256, (n + 1) * 256)
                acc = tmp[k, :, cols] + dot(
                    place[rows_of(k), pl.ds(other, HALF)], xg[p, pl.ds(other, HALF), cols]
                )
                stage[k, :, cols] = scaled(acc, p, k)
            send_piece(p, k, k)

        shared_part(xg[p, pl.ds(mine, HALF), :])

    @pl.loop(0, ND)
    def _(d):
        pltpu.make_async_copy(
            tok.at[:, pl.ds(0, CW)], xg.at[d, pl.ds(me * TD, TD), :], own_sem.at[d]
        ).wait()
        rows = pl.ds(pl.multiple_of(d * CW, CW), CW)

        def part(block):
            sga[...] += dot(block, sg[rows, :])
            sua[...] += dot(block, su[rows, :])

        first_groups(d, part)

    @pl.loop(0, ND)
    def _(d):
        p = d + ND
        pltpu.make_async_copy(
            tok.at[:, pl.ds(0, CW)], xg.at[p, pl.ds(me * TD, TD), :], own_sem.at[p]
        ).wait()
        rows = pl.ds(pl.multiple_of(d * CW, CW), CW)

        def part(block):
            sda[...] += dot(block, sd[rows, :])

        first_groups(p, part)

    s_gate, s_up, s_hid = sga[...], sua[...], sda[...]
    sig = jax.nn.sigmoid(s_gate)
    sdg[...] = (s_hid * s_up * sig * (1.0 + s_gate * (1.0 - sig))).astype(BF)
    sdu[...] = (s_hid * s_gate * sig).astype(BF)

    for j, (h, v) in enumerate(weights):
        pltpu.make_async_copy(h, v, w_sem.at[j]).wait()

    def late_piece(k, p):
        for n in range(3):
            cols = slice(n * 256, (n + 1) * 256)
            acc = dot(place[rows_of(k), :], xg[p, :, cols])
            stage[0, :, cols] = scaled(acc, p, k)
        send_piece(p, k, 0)

    def fetch(k):
        for d in range(ND):
            pltpu.make_async_copy(rb.at[d, rows_of(k), :], xb.at[d], in_sem).start()
            pltpu.make_async_copy(rb.at[ND + d, rows_of(k), :], gb.at[d], in_sem).start()
        wait_for(xb, in_sem)
        wait_for(gb, in_sem)

    def expert(k):
        low_gate = sum(dot_last(xb[d], gin[:, d * CW : (d + 1) * CW]) for d in range(ND)).astype(BF)
        low_up = sum(dot_last(xb[d], uin[:, d * CW : (d + 1) * CW]) for d in range(ND)).astype(BF)

        @pl.loop(0, FF // 256)
        def _(j):
            cols = pl.ds(pl.multiple_of(j * 256, 256), 256)
            gate = sum(dot(xb[d], gw[d * CW : (d + 1) * CW, cols]) for d in range(ND))
            gate = gate + dot(low_gate, gout[:, cols])
            up = sum(dot(xb[d], uw[d * CW : (d + 1) * CW, cols]) for d in range(ND))
            up = up + dot(low_up, uout[:, cols])
            hid = sum(dot_last(gb[d], dw[cols, d * CW : (d + 1) * CW]) for d in range(ND))
            s = jax.nn.sigmoid(gate)
            dg[:, cols] = (hid * up * s * (1.0 + gate * (1.0 - s))).astype(BF)
            du[:, cols] = (hid * gate * s).astype(BF)

        dgv, duv = dg[...], du[...]
        low_dg = dot_last(dgv, gout[...]).astype(BF)
        low_du = dot_last(duv, uout[...]).astype(BF)
        gout_g[...] += dot_first(low_gate, dgv)
        uout_g[...] += dot_first(low_up, duv)
        for d in range(ND):
            cols = slice(d * CW, (d + 1) * CW)
            gin_g[:, cols] += dot_first(low_dg, xb[d])
            uin_g[:, cols] += dot_first(low_du, xb[d])

        @pl.loop(0, ND)
        def _(d):
            for n in range(3):
                rows = pl.ds(pl.multiple_of(d * CW + n * 256, 256), 256)
                acc = dot_last(dg[...], gw[rows, :]) + dot(low_dg, gin[:, rows])
                acc = acc + dot_last(du[...], uw[rows, :]) + dot(low_du, uin[:, rows])
                outb[3 * d + n] = acc.astype(BF)

    def store(k):
        @pl.loop(0, NU)
        def _(u):
            pltpu.make_async_copy(outb.at[u], ob.at[u, rows_of(k), :], o_sem).start()

        wait_for(outb, o_sem)

        @pl.when(k == 0)
        def _():
            back[...] = outb[:, 0:MSG, :]
            pltpu.make_async_copy(back, ret.at[:, pl.ds(0, MSG), :], r_own).start()

    def send_back(k_from, k_to, u_from, u_to):
        @pl.loop(u_from, u_to)
        def _(u):
            @pl.loop(4 * k_from, 4 * k_to)
            def _(i):
                rows = pl.ds(pl.multiple_of(i * MSG, 8), MSG)

                @pl.when(i > 0)
                def _():
                    remote(
                        ob.at[u, rows, :], ret.at[u, rows, :], r_send, r_recv.at[u], peer(i, -1)
                    ).start()

    @pl.loop(FIRST, 4)
    def _(k):
        @pl.loop(0, NP)
        def _(p):
            late_piece(k, p)

    hit_t = hits[...].T
    for b in range(NB):
        place_t[b * TD : (b + 1) * TD, :] = (hit_t * block_row[b : b + 1, :]).astype(BF)

    @pl.loop(0, 4)
    def _(k):
        @pl.when(k == 0)
        def _():
            wait_for(rb.at[:, pl.ds(0, 3 * MSG), :], d_recv.at[0])
            wait_for(rb.at[:, pl.ds(0, MSG), :], d_own)

        @pl.when(k > 0)
        def _():
            wait_for(rb.at[:, pl.ds(0, GR), :], d_recv.at[k])

        fetch(k)
        expert(k)
        store(k)

        @pl.when(k < 3)
        def _():
            send_back(k, k + 1, 0, 3)

        @pl.when(k == 2)
        def _():
            send_back(0, 3, 3, 6)

        @pl.when(k == 3)
        def _():
            send_back(3, 4, 0, 6)
            send_back(0, 4, 6, NU)

    wait_for(ret.at[:, pl.ds(0, MSG), :], r_own)

    def combine(u):
        wide = pl.ds(pl.multiple_of(u * UW, UW), UW)
        wait_for(ret.at[u, pl.ds(0, ROWS - MSG), :], r_recv.at[u])
        cp = pltpu.make_async_copy(ret.at[u], retv, rv_sem)
        cp.start()
        cp.wait()
        csb[u] = dot(place_t[pl.ds(other, HALF), :], retv[...]).astype(BF)
        remote(csb.at[u], crb.at[u], c_send, c_recv.at[u], sibling()).start()
        acc = dot(place_t[pl.ds(mine, HALF), :], retv[...])
        own[u] = acc + (dot_last(sdg[...], sg[wide, :]) + dot_last(sdu[...], su[wide, :]))

    def across(u):
        wait_for(crb.at[u], c_recv.at[u])
        own[u] = own[u] + crb[u].astype(F32)
        for o in (2, 1, 3):
            slot = pl.ds(pl.multiple_of(((x + o) % 4) * TD, TD), TD)
            xsb[u, o - 1] = own[u, slot, :].astype(BF)
            remote(xsb.at[u, o - 1], xrb.at[u, o - 1], x_send, x_recv.at[u], x_peer(o)).start()

    def finish(u):
        wait_for(xrb.at[u], x_recv.at[u])
        total = own[u, pl.ds(pl.multiple_of(x * TD, TD), TD), :]
        for o in range(3):
            total = total + xrb[u, o].astype(F32)
        fin[u] = total.astype(BF)
        wide = pl.ds(pl.multiple_of(u * UW, UW), UW)
        pltpu.make_async_copy(fin.at[u], out.at[:, wide], f_sem).start()

    @pl.loop(0, NU + 2)
    def _(t):
        @pl.when(t < NU)
        def _():
            combine(jnp.minimum(t, NU - 1))

        @pl.when((t > 0) & (t <= NU))
        def _():
            across(jnp.clip(t - 1, 0, NU - 1))

        @pl.when(t > 1)
        def _():
            finish(jnp.maximum(t - 2, 0))

    wait_for(meta_all.at[pl.ds(0, 7)], m_send)
    wait_for(xg.at[:, pl.ds(0, 3 * TD), :], gx_send)
    wait_for(xg.at[:, pl.ds(0, 4 * TD), :], gc_send)
    wait_for(sb.at[:, pl.ds(0, ROWS - MSG), :], d_send)
    wait_for(ob.at[:, pl.ds(0, ROWS - MSG), :], r_send)
    wait_for(csb, c_send)
    wait_for(xsb, x_send)
    wait_for(fin, f_sem)


def hand_over(*refs):
    for j in range(5):
        refs[5 + j][...] = refs[j][...].reshape(refs[5 + j].shape)


def tables():
    r = np.arange(ROWS)
    i, b, s = r // MSG, (r // CAP) % NB, r % CAP
    expand = (np.arange(TD)[None, :] == (b * NPEER + i)[:, None]).astype(np.float32)
    slot_of = np.broadcast_to(s[:, None], (ROWS, TD)).astype(np.float32)
    block_of = np.broadcast_to(b[:, None], (ROWS, TD)).astype(np.float32)
    block_row = (b[None, :] == np.arange(NB)[:, None]).astype(np.float32)
    return expand, slot_of, block_of, block_row


def local(
    tokens,
    output_grad,
    chosen_experts,
    route_weights,
    gate_weight,
    up_weight,
    down_weight,
    gate_adapter_in,
    gate_adapter_out,
    up_adapter_in,
    up_adapter_out,
    shared_gate,
    shared_up,
    shared_down,
):
    expand, slot_of, block_of, block_row = tables()
    any_spec = pl.BlockSpec(memory_space=pl.ANY)
    vmem = pl.BlockSpec(memory_space=pltpu.VMEM)
    rank = gate_adapter_in.shape[1]
    sff = shared_gate.shape[1]
    dma = pltpu.SemaphoreType.DMA
    shape = jax.ShapeDtypeStruct
    outs = pl.pallas_call(
        kernel,
        name="moe_backward",
        out_shape=(
            shape((TD, D), BF),
            shape((rank, D), F32),
            shape((rank, FF), F32),
            shape((rank, D), F32),
            shape((rank, FF), F32),
            shape((NP, ROWS, CW), BF),
            shape((NP, ROWS, CW), BF),
            shape((NU, ROWS, UW), BF),
            shape((NU, ROWS, UW), BF),
        ),
        in_specs=[any_spec] * 2
        + [vmem] * 6
        + [any_spec] * 3
        + [vmem] * 4
        + [any_spec] * 3,
        out_specs=(any_spec, vmem, vmem, vmem, vmem) + (any_spec,) * 4,
        scratch_shapes=[
            pltpu.VMEM((D, FF), BF),
            pltpu.VMEM((D, FF), BF),
            pltpu.VMEM((FF, D), BF),
            pltpu.VMEM((D, sff), BF),
            pltpu.VMEM((D, sff), BF),
            pltpu.VMEM((D, sff), BF),
            pltpu.VMEM((NB, 2, NPEER, TD), F32),
            pltpu.VMEM((NB, 2, NPEER, TD), F32),
            pltpu.VMEM((NP, NB * TD, CW), BF),
            pltpu.VMEM((ROWS, NB * TD), BF),
            pltpu.VMEM((NB * TD, ROWS), BF),
            pltpu.VMEM((ROWS, TD), F32),
            pltpu.VMEM((ROWS, TD), F32),
            pltpu.VMEM((FIRST, GR, CW), F32),
            pltpu.VMEM((FIRST, GR, CW), BF),
            pltpu.VMEM((ND, GR, CW), BF),
            pltpu.VMEM((ND, GR, CW), BF),
            pltpu.VMEM((GR, FF), BF),
            pltpu.VMEM((GR, FF), BF),
            pltpu.VMEM((NU, GR, UW), BF),
            pltpu.VMEM((NP, MSG, CW), BF),
            pltpu.VMEM((NU, MSG, UW), BF),
            pltpu.VMEM((HALF, sff), F32),
            pltpu.VMEM((HALF, sff), F32),
            pltpu.VMEM((HALF, sff), F32),
            pltpu.VMEM((HALF, sff), BF),
            pltpu.VMEM((HALF, sff), BF),
            pltpu.VMEM((ROWS, UW), BF),
            pltpu.VMEM((NU, HALF, UW), F32),
            pltpu.VMEM((NU, HALF, UW), BF),
            pltpu.VMEM((NU, HALF, UW), BF),
            pltpu.VMEM((NU, 3, TD, UW), BF),
            pltpu.VMEM((NU, 3, TD, UW), BF),
            pltpu.VMEM((NU, TD, UW), BF),
            dma((3,)),
            dma,
            dma,
            dma,
            dma,
            dma((NP,)),
            dma,
            dma((NP, 3)),
            dma,
            dma((NP,)),
            dma,
            dma,
            dma((4,)),
            dma,
            dma,
            dma,
            dma,
            dma((NU,)),
            dma,
            dma,
            dma,
            dma((NU,)),
            dma,
            dma((NU,)),
            dma,
        ],
        compiler_params=pltpu.CompilerParams(
            collective_id=0, has_side_effects=True, vmem_limit_bytes=62 << 20
        ),
    )(
        tokens,
        output_grad,
        chosen_experts.T,
        route_weights.T,
        jnp.asarray(expand, BF),
        jnp.asarray(slot_of),
        jnp.asarray(block_of),
        jnp.asarray(block_row),
        gate_weight[0],
        up_weight[0],
        down_weight[0],
        gate_adapter_in[0],
        gate_adapter_out[0],
        up_adapter_in[0],
        up_adapter_out[0],
        shared_gate,
        shared_up,
        shared_down,
    )
    return pl.pallas_call(
        hand_over,
        name="hand_over",
        out_shape=(
            shape((TD, D), BF),
            shape((1, rank, D), F32),
            shape((1, rank, FF), F32),
            shape((1, rank, D), F32),
            shape((1, rank, FF), F32),
        ),
        in_specs=[vmem] * 5,
        out_specs=(vmem,) * 5,
    )(*outs[:5])


def solution(mesh):
    in_specs = (
        (P(("ep", "rep"), None),) * 4 + (P(("ep", "rep"), None, None),) * 7 + (P(None, "rep"),) * 3
    )
    out_specs = (P(("ep", "rep"), None),) + (P(("ep", "rep"), None, None),) * 4
    return jax.shard_map(
        local, mesh=mesh, in_specs=in_specs, out_specs=out_specs, check_vma=False
    )
```

```python
import jax
import jax.numpy as jnp
from jax import lax
from jax.experimental import pallas as pl
from jax.experimental.pallas import tpu as pltpu
from jax.sharding import PartitionSpec as P

MESH = pl.DeviceIdType.MESH
BF = jnp.bfloat16
F32 = jnp.float32

TD = 128
D = 2304
FF = 1024
CAP = 9
NB = 8
NPEER = 16
MSG = NB * CAP
ROWS = NPEER * MSG
GR = 4 * MSG
ND = 3
CW = D // ND
NA = 2
PIECES = ((0, 0, 1), (0, 1, 2), (0, 3, 3), (0, 6, 3), (1, 0, 3), (1, 3, 3), (1, 6, 3))
HALF = 4 * TD
UW = 256
NU = D // UW
FIRST = 3


def dot(a, b):
    return jnp.dot(a, b, preferred_element_type=F32)


def dot_last(a, b):
    return lax.dot_general(a, b, (((1,), (1,)), ((), ())), preferred_element_type=F32)


def dot_first(a, b):
    return lax.dot_general(a, b, (((0,), (0,)), ((), ())), preferred_element_type=F32)


def position():
    e, x = lax.axis_index("ep"), lax.axis_index("rep")
    return e // 8, (e // 2) % 4, e % 2, x


def peer(i, sign):
    z, y, c, x = position()
    oy = i % 4
    oz = (i % 4 + i // 4) % 4
    way = sign * (1 - 2 * c)
    zz = (z + way * oz + 4) % 4
    yy = (y + way * oy + 4) % 4
    return {"ep": (zz * 4 + yy) * 2 + c, "rep": x}


def x_peer(o):
    z, y, c, x = position()
    return {"ep": (z * 4 + y) * 2 + c, "rep": (x + o) % 4}


def member(o):
    z, y, c, x = position()
    return {"ep": (z * 4 + y) * 2 + (c + o // 4) % 2, "rep": (x + o) % 4}


def member_slot(o):
    z, y, c, x = position()
    return ((c + o // 4) % 2) * 4 + (x + o) % 4


def sibling():
    z, y, c, x = position()
    return {"ep": (z * 4 + y) * 2 + 1 - c, "rep": x}


def remote(src, dst, send, recv, device):
    return pltpu.make_async_remote_copy(
        src_ref=src,
        dst_ref=dst,
        send_sem=send,
        recv_sem=recv,
        device_id=device,
        device_id_type=MESH,
    )


def wait_for(ref, sem):
    pltpu.make_async_copy(ref, ref, sem).wait()


def kernel(
    tok,
    grd,
    chosen,
    route,
    gw_h,
    uw_h,
    dw_h,
    gin,
    gout,
    uin,
    uout,
    sg_h,
    su_h,
    sd_h,
    out,
    gin_g,
    gout_g,
    uin_g,
    uout_g,
    sb,
    rb,
    ob,
    ret,
    gw,
    uw,
    dw,
    sg,
    su,
    sd,
    meta,
    meta_all,
    xg,
    place,
    place_t,
    wsl,
    hits,
    tmp,
    stage,
    xb,
    gb,
    dg,
    du,
    outb,
    kept,
    back,
    sga,
    sua,
    sda,
    sdg,
    sdu,
    retv,
    own,
    csb,
    crb,
    xsb,
    xrb,
    fin,
    w_sem,
    s_sem,
    m_send,
    m_recv,
    m_own,
    own_sem,
    gx_send,
    gx_recv,
    gc_send,
    gc_recv,
    st_sem,
    d_send,
    d_recv,
    d_own,
    in_sem,
    o_sem,
    r_send,
    r_recv,
    r_own,
    rv_sem,
    c_send,
    c_recv,
    x_send,
    x_recv,
    f_sem,
):
    z, y, c, x = position()
    me = c * 4 + x

    barrier = pltpu.get_barrier_semaphore()

    @pl.loop(1, NPEER)
    def _(i):
        pl.semaphore_signal(barrier, inc=1, device_id=peer(i, 1), device_id_type=MESH)

    @pl.loop(1, 8)
    def _(o):
        pl.semaphore_signal(barrier, inc=1, device_id=member(o), device_id_type=MESH)

    weights = [(gw_h, gw), (uw_h, uw), (dw_h, dw)]
    shared = [(sg_h, sg), (su_h, su), (sd_h, sd)]

    def piece_of(p):
        a, first, width = PIECES[p]
        cols = pl.ds(first * UW, width * UW)
        return (grd if a else tok).at[:, cols], xg.at[a, pl.ds(me * TD, TD), cols]

    for p in range(len(PIECES)):
        src, dst = piece_of(p)
        pltpu.make_async_copy(src, dst, own_sem.at[p]).start()
    for h, v in shared:
        pltpu.make_async_copy(h, v, s_sem).start()
    for j, (h, v) in enumerate(weights):
        pltpu.make_async_copy(h, v, w_sem.at[j]).start()
    gin_g[...] = jnp.zeros_like(gin_g)
    gout_g[...] = jnp.zeros_like(gout_g)
    uin_g[...] = jnp.zeros_like(uin_g)
    uout_g[...] = jnp.zeros_like(uout_g)
    sga[...] = jnp.zeros_like(sga)
    sua[...] = jnp.zeros_like(sua)
    sda[...] = jnp.zeros_like(sda)

    row_i = lax.broadcasted_iota(jnp.int32, (TD, TD), 0)
    col_i = lax.broadcasted_iota(jnp.int32, (TD, TD), 1)
    group, chip = row_i >> 4, row_i & 15
    way = 1 - 2 * (group >> 2)
    zz = (z + way * ((chip & 3) + (chip >> 2)) + 8) & 3
    yy = (y + way * (chip & 3) + 8) & 3
    ids = (((zz * 4 + yy) * 2 + (group >> 2)) * 4) + (group & 3)
    picked = jnp.zeros((TD, TD), F32)
    weight = jnp.zeros((TD, TD), F32)
    for k in range(chosen.shape[0]):
        same = chosen[k : k + 1, :] == ids
        picked = jnp.where(same, 1.0, picked)
        weight = jnp.where(same, route[k : k + 1, :], weight)
    before = jnp.where(row_i < col_i, 1.0, 0.0).astype(BF)
    count = dot(picked.astype(BF), before)
    meta[:, 0] = jnp.where(picked > 0.0, count, -1.0).reshape(NB, NPEER, TD)
    meta[:, 1] = weight.reshape(NB, NPEER, TD)
    own_meta = pltpu.make_async_copy(meta.at[me], meta_all.at[me], m_own)
    own_meta.start()

    pl.semaphore_wait(barrier, NPEER - 1 + 7)

    @pl.loop(1, 8)
    def _(o):
        remote(meta.at[member_slot(o)], meta_all.at[me], m_send, m_recv, member(o)).start()

    for p in range(len(PIECES)):
        src, dst = piece_of(p)
        for o in (1, 3, 2):
            remote(src, dst, gx_send, gx_recv.at[p, o - 1], x_peer(o)).start()
        remote(src, dst, gc_send, gc_recv.at[p], sibling()).start()

    row = lax.broadcasted_iota(jnp.int32, (ROWS, TD), 0)
    lane = lax.broadcasted_iota(jnp.int32, (ROWS, TD), 1)
    nine = (row * 7282) >> 16
    slot_of = (row - CAP * nine).astype(F32)
    block_of = nine & 7
    spread = jnp.where(lane == block_of * NPEER + (nine >> 3), 1.0, 0.0).astype(BF)

    own_meta.wait()
    wait_for(meta_all.at[pl.ds(0, 7)], m_recv)

    code = meta_all[:, 0].reshape(TD, TD).astype(BF)
    hit = jnp.where(dot(spread, code) == slot_of, 1.0, 0.0)
    w_all = meta_all[:, 1].reshape(TD, TD)
    w_hi = w_all.astype(BF)
    left = w_all - w_hi.astype(F32)
    w_mid = left.astype(BF)
    w_lo = (left - w_mid.astype(F32)).astype(BF)
    w_row = (dot(spread, w_hi) + dot(spread, w_mid)) + dot(spread, w_lo)
    wsl[...] = jnp.broadcast_to(jnp.sum(w_row * hit, axis=1, keepdims=True), (ROWS, TD))
    hits[...] = hit
    for b in range(NB):
        place[:, b * TD : (b + 1) * TD] = jnp.where(block_of == b, hit, 0.0).astype(BF)

    wait_shared = [pltpu.make_async_copy(h, v, s_sem) for h, v in shared]
    for cp in wait_shared:
        cp.wait()

    mine = pl.multiple_of(c * HALF, HALF)
    other = pl.multiple_of((1 - c) * HALF, HALF)

    def rows_of(k):
        return pl.ds(pl.multiple_of(k * GR, 8), GR)

    def send_piece(a, cols, width, k, slot):
        filled = stage.at[slot, :, pl.ds(0, width)]
        cp = pltpu.make_async_copy(filled, sb.at[a, rows_of(k), cols], st_sem)
        cp.start()
        cp.wait()

        @pl.loop(0, 4)
        def _(j):
            i = k * 4 + j
            rows = pl.ds(pl.multiple_of(i * MSG, 8), MSG)

            @pl.when(i > 0)
            def _():
                remote(
                    sb.at[a, rows, cols], rb.at[a, rows, cols], d_send, d_recv.at[k], peer(i, 1)
                ).start()

            @pl.when(i == 0)
            def _():
                kept[a, :, cols] = stage[slot, 0:MSG, 0:width]
                pltpu.make_async_copy(kept.at[a, :, cols], rb.at[a, rows, cols], d_own).start()

    def scaled(acc, a, k):
        scale = jnp.where(a == 0, 1.0, wsl[rows_of(k), :][:, 0:1])
        return (acc * scale).astype(BF)

    def units(first, n):
        return pl.ds(pl.multiple_of((first + n) * UW, UW), UW)

    def first_groups(p, a, first, count):
        width = count * UW
        cols = pl.ds(pl.multiple_of(first * UW, UW), width)
        own_block = xg.at[a, pl.ds(me * TD, TD), cols]
        wait_for(own_block, own_sem.at[p])
        for o in (1, 3, 2):
            slot = pl.ds(pl.multiple_of((c * 4 + (x + 4 - o) % 4) * TD, TD), TD)
            block = xg.at[a, slot, cols]
            wait_for(block, gx_recv.at[p, o - 1])
            remote(block, block, gc_send, gc_recv.at[p], sibling()).start()

        @pl.loop(0, FIRST)
        def _(k):
            for n in range(count):
                tmp[k, :, n * UW : (n + 1) * UW] = dot(
                    place[rows_of(k), pl.ds(mine, HALF)], xg[a, pl.ds(mine, HALF), units(first, n)]
                )

        wait_for(xg.at[a, pl.ds(other, HALF), cols], gc_recv.at[p])

        @pl.loop(0, FIRST)
        def _(k):
            for n in range(count):
                here = slice(n * UW, (n + 1) * UW)
                acc = tmp[k, :, here] + dot(
                    place[rows_of(k), pl.ds(other, HALF)],
                    xg[a, pl.ds(other, HALF), units(first, n)],
                )
                stage[k, :, here] = scaled(acc, a, k)
            send_piece(a, cols, width, k, k)

        for n in range(count):
            block = xg[a, pl.ds(mine, HALF), units(first, n)]
            if a == 0:
                sga[...] += dot(block, sg[units(first, n), :])
                sua[...] += dot(block, su[units(first, n), :])
            else:
                sda[...] += dot(block, sd[units(first, n), :])

    first_groups(0, *PIECES[0])
    first_groups(1, *PIECES[1])

    @pl.loop(0, 2)
    def _(j):
        first_groups(2 + j, 0, 3 + 3 * j, 3)

    @pl.loop(0, 3)
    def _(j):
        first_groups(4 + j, 1, 3 * j, 3)

    s_gate, s_up, s_hid = sga[...], sua[...], sda[...]
    sig = jax.nn.sigmoid(s_gate)
    sdg[...] = (s_hid * s_up * sig * (1.0 + s_gate * (1.0 - sig))).astype(BF)
    sdu[...] = (s_hid * s_gate * sig).astype(BF)

    for j, (h, v) in enumerate(weights):
        pltpu.make_async_copy(h, v, w_sem.at[j]).wait()

    def late_piece(k, a, d):
        for n in range(3):
            acc = dot(place[rows_of(k), :], xg[a, :, units(3 * d, n)])
            stage[0, :, n * UW : (n + 1) * UW] = scaled(acc, a, k)
        send_piece(a, pl.ds(pl.multiple_of(d * CW, CW), CW), CW, k, 0)

    def fetch(k):
        pltpu.make_async_copy(rb.at[0, rows_of(k), :], xb, in_sem).start()
        pltpu.make_async_copy(rb.at[1, rows_of(k), :], gb, in_sem).start()
        wait_for(xb, in_sem)
        wait_for(gb, in_sem)

    def expert(k):
        low_gate = sum(dot_last(xb[:, d * CW : (d + 1) * CW], gin[:, d * CW : (d + 1) * CW]) for d in range(ND)).astype(BF)
        low_up = sum(dot_last(xb[:, d * CW : (d + 1) * CW], uin[:, d * CW : (d + 1) * CW]) for d in range(ND)).astype(BF)

        @pl.loop(0, FF // 256)
        def _(j):
            cols = pl.ds(pl.multiple_of(j * 256, 256), 256)
            gate = sum(dot(xb[:, d * CW : (d + 1) * CW], gw[d * CW : (d + 1) * CW, cols]) for d in range(ND))
            gate = gate + dot(low_gate, gout[:, cols])
            up = sum(dot(xb[:, d * CW : (d + 1) * CW], uw[d * CW : (d + 1) * CW, cols]) for d in range(ND))
            up = up + dot(low_up, uout[:, cols])
            hid = sum(dot_last(gb[:, d * CW : (d + 1) * CW], dw[cols, d * CW : (d + 1) * CW]) for d in range(ND))
            s = jax.nn.sigmoid(gate)
            dg[:, cols] = (hid * up * s * (1.0 + gate * (1.0 - s))).astype(BF)
            du[:, cols] = (hid * gate * s).astype(BF)

        dgv, duv = dg[...], du[...]
        low_dg = dot_last(dgv, gout[...]).astype(BF)
        low_du = dot_last(duv, uout[...]).astype(BF)
        gout_g[...] += dot_first(low_gate, dgv)
        uout_g[...] += dot_first(low_up, duv)
        for d in range(ND):
            cols = slice(d * CW, (d + 1) * CW)
            gin_g[:, cols] += dot_first(low_dg, xb[:, d * CW : (d + 1) * CW])
            uin_g[:, cols] += dot_first(low_du, xb[:, d * CW : (d + 1) * CW])

        @pl.loop(0, ND)
        def _(d):
            for n in range(3):
                rows = pl.ds(pl.multiple_of(d * CW + n * 256, 256), 256)
                acc = dot_last(dg[...], gw[rows, :]) + dot(low_dg, gin[:, rows])
                acc = acc + dot_last(du[...], uw[rows, :]) + dot(low_du, uin[:, rows])
                outb[3 * d + n] = acc.astype(BF)

    def store(k):
        @pl.loop(0, NU)
        def _(u):
            pltpu.make_async_copy(outb.at[u], ob.at[u, rows_of(k), :], o_sem).start()

        wait_for(outb, o_sem)

        @pl.when(k == 0)
        def _():
            back[...] = outb[:, 0:MSG, :]
            pltpu.make_async_copy(back, ret.at[:, pl.ds(0, MSG), :], r_own).start()

    def send_back(k_from, k_to, u_from, u_to):
        @pl.loop(u_from, u_to)
        def _(u):
            @pl.loop(4 * k_from, 4 * k_to)
            def _(i):
                rows = pl.ds(pl.multiple_of(i * MSG, 8), MSG)

                @pl.when(i > 0)
                def _():
                    remote(
                        ob.at[u, rows, :], ret.at[u, rows, :], r_send, r_recv.at[u], peer(i, -1)
                    ).start()

    @pl.loop(FIRST, 4)
    def _(k):
        @pl.loop(0, NA * ND)
        def _(p):
            late_piece(k, p // ND, p % ND)

    hit_t = hits[...].T
    block_row = ((lax.broadcasted_iota(jnp.int32, (TD, ROWS), 1) * 7282) >> 16) & 7
    for b in range(NB):
        place_t[b * TD : (b + 1) * TD, :] = jnp.where(block_row == b, hit_t, 0.0).astype(BF)

    @pl.loop(0, 4)
    def _(k):
        @pl.when(k == 0)
        def _():
            wait_for(rb.at[:, pl.ds(0, 3 * MSG), :], d_recv.at[0])
            wait_for(rb.at[:, pl.ds(0, MSG), :], d_own)

        @pl.when(k > 0)
        def _():
            wait_for(rb.at[:, pl.ds(0, GR), :], d_recv.at[k])

        fetch(k)
        expert(k)
        store(k)

        @pl.when(k < 3)
        def _():
            send_back(k, k + 1, 0, 3)

        @pl.when(k == 2)
        def _():
            send_back(0, 3, 3, 6)

        @pl.when(k == 3)
        def _():
            send_back(3, 4, 0, 6)

    wait_for(ret.at[:, pl.ds(0, MSG), :], r_own)

    def combine(u):
        wide = pl.ds(pl.multiple_of(u * UW, UW), UW)
        wait_for(ret.at[u, pl.ds(0, ROWS - MSG), :], r_recv.at[u])
        cp = pltpu.make_async_copy(ret.at[u], retv, rv_sem)
        cp.start()
        cp.wait()
        csb[u] = dot(place_t[pl.ds(other, HALF), :], retv[...]).astype(BF)
        remote(csb.at[u], crb.at[u], c_send, c_recv.at[u], sibling()).start()
        acc = dot(place_t[pl.ds(mine, HALF), :], retv[...])
        own[u] = acc + (dot_last(sdg[...], sg[wide, :]) + dot_last(sdu[...], su[wide, :]))

    def across(u):
        wait_for(crb.at[u], c_recv.at[u])
        own[u] = own[u] + crb[u].astype(F32)
        for o in (2, 1, 3):
            slot = pl.ds(pl.multiple_of(((x + o) % 4) * TD, TD), TD)
            xsb[u, o - 1] = own[u, slot, :].astype(BF)
            remote(xsb.at[u, o - 1], xrb.at[u, o - 1], x_send, x_recv.at[u], x_peer(o)).start()

    def finish(u):
        wait_for(xrb.at[u], x_recv.at[u])
        total = own[u, pl.ds(pl.multiple_of(x * TD, TD), TD), :]
        for o in range(3):
            total = total + xrb[u, o].astype(F32)
        fin[u] = total.astype(BF)
        wide = pl.ds(pl.multiple_of(u * UW, UW), UW)
        pltpu.make_async_copy(fin.at[u], out.at[:, wide], f_sem).start()

    @pl.loop(0, NU + 2)
    def _(t):
        @pl.when((t == 1) | (t == 3) | (t == 5))
        def _():
            unit = jnp.clip((t + 11) // 2, 6, 8)
            send_back(0, 4, unit, unit + 1)

        @pl.when(t < NU)
        def _():
            combine(jnp.minimum(t, NU - 1))

        @pl.when((t > 0) & (t <= NU))
        def _():
            across(jnp.clip(t - 1, 0, NU - 1))

        @pl.when(t > 1)
        def _():
            finish(jnp.maximum(t - 2, 0))

    wait_for(meta_all.at[pl.ds(0, 7)], m_send)
    wait_for(xg.at[:, pl.ds(0, 3 * TD), :], gx_send)
    wait_for(xg.at[:, pl.ds(0, 4 * TD), :], gc_send)
    wait_for(sb.at[:, pl.ds(0, ROWS - MSG), :], d_send)
    wait_for(ob.at[:, pl.ds(0, ROWS - MSG), :], r_send)
    wait_for(csb, c_send)
    wait_for(xsb, x_send)
    wait_for(fin, f_sem)


def hand_over(*refs):
    for j in range(5):
        refs[5 + j][...] = refs[j][...].reshape(refs[5 + j].shape)


def local(
    tokens,
    output_grad,
    chosen_experts,
    route_weights,
    gate_weight,
    up_weight,
    down_weight,
    gate_adapter_in,
    gate_adapter_out,
    up_adapter_in,
    up_adapter_out,
    shared_gate,
    shared_up,
    shared_down,
):
    any_spec = pl.BlockSpec(memory_space=pl.ANY)
    vmem = pl.BlockSpec(memory_space=pltpu.VMEM)
    rank = gate_adapter_in.shape[1]
    sff = shared_gate.shape[1]
    dma = pltpu.SemaphoreType.DMA
    shape = jax.ShapeDtypeStruct
    outs = pl.pallas_call(
        kernel,
        name="moe_backward",
        out_shape=(
            shape((TD, D), BF),
            shape((rank, D), F32),
            shape((rank, FF), F32),
            shape((rank, D), F32),
            shape((rank, FF), F32),
            shape((NA, ROWS, D), BF),
            shape((NA, ROWS, D), BF),
            shape((NU, ROWS, UW), BF),
            shape((NU, ROWS, UW), BF),
        ),
        in_specs=[any_spec] * 2
        + [vmem] * 2
        + [any_spec] * 3
        + [vmem] * 4
        + [any_spec] * 3,
        out_specs=(any_spec, vmem, vmem, vmem, vmem) + (any_spec,) * 4,
        scratch_shapes=[
            pltpu.VMEM((D, FF), BF),
            pltpu.VMEM((D, FF), BF),
            pltpu.VMEM((FF, D), BF),
            pltpu.VMEM((D, sff), BF),
            pltpu.VMEM((D, sff), BF),
            pltpu.VMEM((D, sff), BF),
            pltpu.VMEM((NB, 2, NPEER, TD), F32),
            pltpu.VMEM((NB, 2, NPEER, TD), F32),
            pltpu.VMEM((NA, NB * TD, D), BF),
            pltpu.VMEM((ROWS, NB * TD), BF),
            pltpu.VMEM((NB * TD, ROWS), BF),
            pltpu.VMEM((ROWS, TD), F32),
            pltpu.VMEM((ROWS, TD), F32),
            pltpu.VMEM((FIRST, GR, CW), F32),
            pltpu.VMEM((FIRST, GR, CW), BF),
            pltpu.VMEM((GR, D), BF),
            pltpu.VMEM((GR, D), BF),
            pltpu.VMEM((GR, FF), BF),
            pltpu.VMEM((GR, FF), BF),
            pltpu.VMEM((NU, GR, UW), BF),
            pltpu.VMEM((NA, MSG, D), BF),
            pltpu.VMEM((NU, MSG, UW), BF),
            pltpu.VMEM((HALF, sff), F32),
            pltpu.VMEM((HALF, sff), F32),
            pltpu.VMEM((HALF, sff), F32),
            pltpu.VMEM((HALF, sff), BF),
            pltpu.VMEM((HALF, sff), BF),
            pltpu.VMEM((ROWS, UW), BF),
            pltpu.VMEM((NU, HALF, UW), F32),
            pltpu.VMEM((NU, HALF, UW), BF),
            pltpu.VMEM((NU, HALF, UW), BF),
            pltpu.VMEM((NU, 3, TD, UW), BF),
            pltpu.VMEM((NU, 3, TD, UW), BF),
            pltpu.VMEM((NU, TD, UW), BF),
            dma((3,)),
            dma,
            dma,
            dma,
            dma,
            dma((len(PIECES),)),
            dma,
            dma((len(PIECES), 3)),
            dma,
            dma((len(PIECES),)),
            dma,
            dma,
            dma((4,)),
            dma,
            dma,
            dma,
            dma,
            dma((NU,)),
            dma,
            dma,
            dma,
            dma((NU,)),
            dma,
            dma((NU,)),
            dma,
        ],
        compiler_params=pltpu.CompilerParams(
            collective_id=0, has_side_effects=True, vmem_limit_bytes=62 << 20
        ),
    )(
        tokens,
        output_grad,
        chosen_experts.T,
        route_weights.T,
        gate_weight[0],
        up_weight[0],
        down_weight[0],
        gate_adapter_in[0],
        gate_adapter_out[0],
        up_adapter_in[0],
        up_adapter_out[0],
        shared_gate,
        shared_up,
        shared_down,
    )
    return pl.pallas_call(
        hand_over,
        name="hand_over",
        out_shape=(
            shape((TD, D), BF),
            shape((1, rank, D), F32),
            shape((1, rank, FF), F32),
            shape((1, rank, D), F32),
            shape((1, rank, FF), F32),
        ),
        in_specs=[vmem] * 5,
        out_specs=(vmem,) * 5,
    )(*outs[:5])


def solution(mesh):
    in_specs = (
        (P(("ep", "rep"), None),) * 4 + (P(("ep", "rep"), None, None),) * 7 + (P(None, "rep"),) * 3
    )
    out_specs = (P(("ep", "rep"), None),) + (P(("ep", "rep"), None, None),) * 4
    return jax.shard_map(
        local, mesh=mesh, in_specs=in_specs, out_specs=out_specs, check_vma=False
    )
```

```python
import jax
import jax.numpy as jnp
from jax import lax
from jax.experimental import pallas as pl
from jax.experimental.pallas import tpu as pltpu
from jax.sharding import PartitionSpec as P

MESH = pl.DeviceIdType.MESH
BF = jnp.bfloat16
F32 = jnp.float32

TD = 128
D = 2304
FF = 1024
CAP = 9
NB = 8
NPEER = 16
MSG = NB * CAP
ROWS = NPEER * MSG
GR = 4 * MSG
ND = 3
CW = D // ND
NA = 2
PIECES = ((0, 0, 1), (0, 1, 2), (0, 3, 3), (0, 6, 3), (1, 0, 3), (1, 3, 3), (1, 6, 3))
HALF = 4 * TD
UW = 256
NU = D // UW
FIRST = 2


def dot(a, b):
    return jnp.dot(a, b, preferred_element_type=F32)


def dot_last(a, b):
    return lax.dot_general(a, b, (((1,), (1,)), ((), ())), preferred_element_type=F32)


def dot_first(a, b):
    return lax.dot_general(a, b, (((0,), (0,)), ((), ())), preferred_element_type=F32)


def position():
    e, x = lax.axis_index("ep"), lax.axis_index("rep")
    return e // 8, (e // 2) % 4, e % 2, x


def peer(i, sign):
    z, y, c, x = position()
    oy = i % 4
    oz = (i % 4 + i // 4) % 4
    way = sign * (1 - 2 * c)
    zz = (z + way * oz + 4) % 4
    yy = (y + way * oy + 4) % 4
    return {"ep": (zz * 4 + yy) * 2 + c, "rep": x}


def x_peer(o):
    z, y, c, x = position()
    return {"ep": (z * 4 + y) * 2 + c, "rep": (x + o) % 4}


def member(o):
    z, y, c, x = position()
    return {"ep": (z * 4 + y) * 2 + (c + o // 4) % 2, "rep": (x + o) % 4}


def member_slot(o):
    z, y, c, x = position()
    return ((c + o // 4) % 2) * 4 + (x + o) % 4


def sibling():
    z, y, c, x = position()
    return {"ep": (z * 4 + y) * 2 + 1 - c, "rep": x}


def remote(src, dst, send, recv, device):
    return pltpu.make_async_remote_copy(
        src_ref=src,
        dst_ref=dst,
        send_sem=send,
        recv_sem=recv,
        device_id=device,
        device_id_type=MESH,
    )


def wait_for(ref, sem):
    pltpu.make_async_copy(ref, ref, sem).wait()


def kernel(
    tok,
    grd,
    chosen,
    route,
    gw_h,
    uw_h,
    dw_h,
    gin,
    gout,
    uin,
    uout,
    sg_h,
    su_h,
    sd_h,
    out,
    gin_g,
    gout_g,
    uin_g,
    uout_g,
    sb,
    rb,
    ob,
    ret,
    gw,
    uw,
    dw,
    sg,
    su,
    sd,
    meta,
    meta_all,
    xg,
    place,
    place_t,
    wsl,
    hits,
    tmp,
    stage,
    xb,
    gb,
    dg,
    du,
    outb,
    kept,
    back,
    sga,
    sua,
    sda,
    sdg,
    sdu,
    retv,
    own,
    csb,
    crb,
    xsb,
    xrb,
    fin,
    w_sem,
    s_sem,
    m_send,
    m_recv,
    m_own,
    own_sem,
    gx_send,
    gx_recv,
    gc_send,
    gc_recv,
    st_sem,
    d_send,
    d_recv,
    d_own,
    in_sem,
    o_sem,
    r_send,
    r_recv,
    r_own,
    rv_sem,
    c_send,
    c_recv,
    x_send,
    x_recv,
    f_sem,
):
    z, y, c, x = position()
    me = c * 4 + x

    barrier = pltpu.get_barrier_semaphore()

    @pl.loop(1, NPEER)
    def _(i):
        pl.semaphore_signal(barrier, inc=1, device_id=peer(i, 1), device_id_type=MESH)

    @pl.loop(1, 8)
    def _(o):
        pl.semaphore_signal(barrier, inc=1, device_id=member(o), device_id_type=MESH)

    weights = [(gw_h, gw), (uw_h, uw), (dw_h, dw)]
    shared = [(sg_h, sg), (su_h, su), (sd_h, sd)]

    def piece_of(p):
        a, first, width = PIECES[p]
        cols = pl.ds(first * UW, width * UW)
        return (grd if a else tok).at[:, cols], xg.at[a, pl.ds(me * TD, TD), cols]

    for p in range(len(PIECES)):
        src, dst = piece_of(p)
        pltpu.make_async_copy(src, dst, own_sem.at[p]).start()
    for h, v in shared:
        pltpu.make_async_copy(h, v, s_sem).start()
    for j, (h, v) in enumerate(weights):
        pltpu.make_async_copy(h, v, w_sem.at[j]).start()
    gin_g[...] = jnp.zeros_like(gin_g)
    gout_g[...] = jnp.zeros_like(gout_g)
    uin_g[...] = jnp.zeros_like(uin_g)
    uout_g[...] = jnp.zeros_like(uout_g)
    sga[...] = jnp.zeros_like(sga)
    sua[...] = jnp.zeros_like(sua)
    sda[...] = jnp.zeros_like(sda)

    row_i = lax.broadcasted_iota(jnp.int32, (TD, TD), 0)
    col_i = lax.broadcasted_iota(jnp.int32, (TD, TD), 1)
    group, chip = row_i >> 4, row_i & 15
    way = 1 - 2 * (group >> 2)
    zz = (z + way * ((chip & 3) + (chip >> 2)) + 8) & 3
    yy = (y + way * (chip & 3) + 8) & 3
    ids = (((zz * 4 + yy) * 2 + (group >> 2)) * 4) + (group & 3)
    picked = jnp.zeros((TD, TD), F32)
    weight = jnp.zeros((TD, TD), F32)
    for k in range(chosen.shape[0]):
        same = chosen[k : k + 1, :] == ids
        picked = jnp.where(same, 1.0, picked)
        weight = jnp.where(same, route[k : k + 1, :], weight)
    before = jnp.where(row_i < col_i, 1.0, 0.0).astype(BF)
    count = dot(picked.astype(BF), before)
    meta[:, 0] = jnp.where(picked > 0.0, count, -1.0).reshape(NB, NPEER, TD)
    meta[:, 1] = weight.reshape(NB, NPEER, TD)
    own_meta = pltpu.make_async_copy(meta.at[me], meta_all.at[me], m_own)
    own_meta.start()

    pl.semaphore_wait(barrier, NPEER - 1 + 7)

    @pl.loop(1, 8)
    def _(o):
        remote(meta.at[member_slot(o)], meta_all.at[me], m_send, m_recv, member(o)).start()

    for p in range(len(PIECES)):
        src, dst = piece_of(p)
        for o in (1, 3, 2):
            remote(src, dst, gx_send, gx_recv.at[p, o - 1], x_peer(o)).start()
        remote(src, dst, gc_send, gc_recv.at[p], sibling()).start()

    def message_rows():
        row = lax.broadcasted_iota(jnp.int32, (ROWS, TD), 0)
        lane = lax.broadcasted_iota(jnp.int32, (ROWS, TD), 1)
        nine = (row * 7282) >> 16
        slot = (row - CAP * nine).astype(F32)
        block = nine & 7
        spread = jnp.where(lane == block * NPEER + (nine >> 3), 1.0, 0.0).astype(BF)
        return spread, block, slot

    spread, block_of, slot_of = message_rows()

    own_meta.wait()
    wait_for(meta_all.at[pl.ds(0, 7)], m_recv)

    code = meta_all[:, 0].reshape(TD, TD).astype(BF)
    hit = jnp.where(dot(spread, code) == slot_of, 1.0, 0.0)
    hits[...] = hit
    for b in range(NB):
        place[:, b * TD : (b + 1) * TD] = jnp.where(block_of == b, hit, 0.0).astype(BF)

    wait_shared = [pltpu.make_async_copy(h, v, s_sem) for h, v in shared]
    for cp in wait_shared:
        cp.wait()

    mine = pl.multiple_of(c * HALF, HALF)
    other = pl.multiple_of((1 - c) * HALF, HALF)

    def rows_of(k):
        return pl.ds(pl.multiple_of(k * GR, 8), GR)

    def send_piece(a, cols, width, k, slot):
        filled = stage.at[slot, :, pl.ds(0, width)]
        cp = pltpu.make_async_copy(filled, sb.at[a, rows_of(k), cols], st_sem)
        cp.start()
        cp.wait()

        @pl.loop(0, 4)
        def _(j):
            i = k * 4 + j
            rows = pl.ds(pl.multiple_of(i * MSG, 8), MSG)

            @pl.when(i > 0)
            def _():
                remote(
                    sb.at[a, rows, cols], rb.at[a, rows, cols], d_send, d_recv.at[k], peer(i, 1)
                ).start()

            @pl.when(i == 0)
            def _():
                kept[a, :, cols] = stage[slot, 0:MSG, 0:width]
                pltpu.make_async_copy(kept.at[a, :, cols], rb.at[a, rows, cols], d_own).start()

    def scaled(acc, a, k):
        if isinstance(a, int) and a == 0:
            return acc.astype(BF)
        scale = jnp.where(a == 0, 1.0, wsl[rows_of(k), :][:, 0:1])
        return (acc * scale).astype(BF)

    def units(first, n):
        return pl.ds(pl.multiple_of((first + n) * UW, UW), UW)

    def first_groups(p, a, first, count):
        width = count * UW
        cols = pl.ds(pl.multiple_of(first * UW, UW), width)
        own_block = xg.at[a, pl.ds(me * TD, TD), cols]
        wait_for(own_block, own_sem.at[p])
        for o in (1, 3, 2):
            slot = pl.ds(pl.multiple_of((c * 4 + (x + 4 - o) % 4) * TD, TD), TD)
            block = xg.at[a, slot, cols]
            wait_for(block, gx_recv.at[p, o - 1])
            remote(block, block, gc_send, gc_recv.at[p], sibling()).start()

        @pl.loop(0, FIRST)
        def _(k):
            for n in range(count):
                tmp[k, :, n * UW : (n + 1) * UW] = dot(
                    place[rows_of(k), pl.ds(mine, HALF)], xg[a, pl.ds(mine, HALF), units(first, n)]
                )

        wait_for(xg.at[a, pl.ds(other, HALF), cols], gc_recv.at[p])

        @pl.loop(0, FIRST)
        def _(k):
            for n in range(count):
                here = slice(n * UW, (n + 1) * UW)
                acc = tmp[k, :, here] + dot(
                    place[rows_of(k), pl.ds(other, HALF)],
                    xg[a, pl.ds(other, HALF), units(first, n)],
                )
                stage[k, :, here] = scaled(acc, a, k)
            send_piece(a, cols, width, k, k)

        for n in range(count):
            block = xg[a, pl.ds(mine, HALF), units(first, n)]
            if a == 0:
                sga[...] += dot(block, sg[units(first, n), :])
                sua[...] += dot(block, su[units(first, n), :])
            else:
                sda[...] += dot(block, sd[units(first, n), :])

    first_groups(0, *PIECES[0])
    first_groups(1, *PIECES[1])

    @pl.loop(0, 2)
    def _(j):
        first_groups(2 + j, 0, 3 + 3 * j, 3)

    again = message_rows()[0]
    w_all = meta_all[:, 1].reshape(TD, TD)
    w_hi = w_all.astype(BF)
    left = w_all - w_hi.astype(F32)
    w_mid = left.astype(BF)
    w_lo = (left - w_mid.astype(F32)).astype(BF)
    w_row = (dot(again, w_hi) + dot(again, w_mid)) + dot(again, w_lo)
    wsl[...] = jnp.broadcast_to(jnp.sum(w_row * hits[...], axis=1, keepdims=True), (ROWS, TD))

    @pl.loop(0, 3)
    def _(j):
        first_groups(4 + j, 1, 3 * j, 3)

    s_gate, s_up, s_hid = sga[...], sua[...], sda[...]
    sig = jax.nn.sigmoid(s_gate)
    sdg[...] = (s_hid * s_up * sig * (1.0 + s_gate * (1.0 - sig))).astype(BF)
    sdu[...] = (s_hid * s_gate * sig).astype(BF)

    for j, (h, v) in enumerate(weights):
        pltpu.make_async_copy(h, v, w_sem.at[j]).wait()

    def late_piece(k, a, d):
        for n in range(3):
            acc = dot(place[rows_of(k), :], xg[a, :, units(3 * d, n)])
            stage[0, :, n * UW : (n + 1) * UW] = scaled(acc, a, k)
        send_piece(a, pl.ds(pl.multiple_of(d * CW, CW), CW), CW, k, 0)

    def fetch(k):
        pltpu.make_async_copy(rb.at[0, rows_of(k), :], xb, in_sem).start()
        pltpu.make_async_copy(rb.at[1, rows_of(k), :], gb, in_sem).start()
        wait_for(xb, in_sem)
        wait_for(gb, in_sem)

    def expert(k):
        low_gate = sum(dot_last(xb[:, d * CW : (d + 1) * CW], gin[:, d * CW : (d + 1) * CW]) for d in range(ND)).astype(BF)
        low_up = sum(dot_last(xb[:, d * CW : (d + 1) * CW], uin[:, d * CW : (d + 1) * CW]) for d in range(ND)).astype(BF)

        @pl.loop(0, FF // 256)
        def _(j):
            cols = pl.ds(pl.multiple_of(j * 256, 256), 256)
            gate = sum(dot(xb[:, d * CW : (d + 1) * CW], gw[d * CW : (d + 1) * CW, cols]) for d in range(ND))
            gate = gate + dot(low_gate, gout[:, cols])
            up = sum(dot(xb[:, d * CW : (d + 1) * CW], uw[d * CW : (d + 1) * CW, cols]) for d in range(ND))
            up = up + dot(low_up, uout[:, cols])
            hid = sum(dot_last(gb[:, d * CW : (d + 1) * CW], dw[cols, d * CW : (d + 1) * CW]) for d in range(ND))
            s = jax.nn.sigmoid(gate)
            dg[:, cols] = (hid * up * s * (1.0 + gate * (1.0 - s))).astype(BF)
            du[:, cols] = (hid * gate * s).astype(BF)

        dgv, duv = dg[...], du[...]
        low_dg = dot_last(dgv, gout[...]).astype(BF)
        low_du = dot_last(duv, uout[...]).astype(BF)
        gout_g[...] += dot_first(low_gate, dgv)
        uout_g[...] += dot_first(low_up, duv)
        for d in range(ND):
            cols = slice(d * CW, (d + 1) * CW)
            gin_g[:, cols] += dot_first(low_dg, xb[:, d * CW : (d + 1) * CW])
            uin_g[:, cols] += dot_first(low_du, xb[:, d * CW : (d + 1) * CW])

        @pl.loop(0, ND)
        def _(d):
            for n in range(3):
                rows = pl.ds(pl.multiple_of(d * CW + n * 256, 256), 256)
                acc = dot_last(dg[...], gw[rows, :]) + dot(low_dg, gin[:, rows])
                acc = acc + dot_last(du[...], uw[rows, :]) + dot(low_du, uin[:, rows])
                outb[3 * d + n] = acc.astype(BF)

    def store(k):
        @pl.loop(0, NU)
        def _(u):
            pltpu.make_async_copy(outb.at[u], ob.at[u, rows_of(k), :], o_sem).start()

        wait_for(outb, o_sem)

        @pl.when(k == 0)
        def _():
            back[...] = outb[:, 0:MSG, :]
            pltpu.make_async_copy(back, ret.at[:, pl.ds(0, MSG), :], r_own).start()

    def send_back(k_from, k_to, u_from, u_to):
        @pl.loop(u_from, u_to)
        def _(u):
            @pl.loop(4 * k_from, 4 * k_to)
            def _(i):
                rows = pl.ds(pl.multiple_of(i * MSG, 8), MSG)

                @pl.when(i > 0)
                def _():
                    remote(
                        ob.at[u, rows, :], ret.at[u, rows, :], r_send, r_recv.at[u], peer(i, -1)
                    ).start()

    @pl.loop(FIRST, 4)
    def _(k):
        @pl.loop(0, NA * ND)
        def _(p):
            late_piece(k, p // ND, p % ND)

    hit_t = hits[...].T
    block_row = ((lax.broadcasted_iota(jnp.int32, (TD, ROWS), 1) * 7282) >> 16) & 7
    for b in range(NB):
        place_t[b * TD : (b + 1) * TD, :] = jnp.where(block_row == b, hit_t, 0.0).astype(BF)

    @pl.loop(0, 4)
    def _(k):
        @pl.when(k == 0)
        def _():
            wait_for(rb.at[:, pl.ds(0, 3 * MSG), :], d_recv.at[0])
            wait_for(rb.at[:, pl.ds(0, MSG), :], d_own)

        @pl.when(k > 0)
        def _():
            wait_for(rb.at[:, pl.ds(0, GR), :], d_recv.at[k])

        fetch(k)
        expert(k)
        store(k)

        @pl.when(k < 3)
        def _():
            send_back(k, k + 1, 0, 3)

        @pl.when(k == 2)
        def _():
            send_back(0, 3, 3, 6)

        @pl.when(k == 3)
        def _():
            send_back(3, 4, 0, 6)

    wait_for(ret.at[:, pl.ds(0, MSG), :], r_own)

    def combine(u):
        wide = pl.ds(pl.multiple_of(u * UW, UW), UW)
        wait_for(ret.at[u, pl.ds(0, ROWS - MSG), :], r_recv.at[u])
        cp = pltpu.make_async_copy(ret.at[u], retv, rv_sem)
        cp.start()
        cp.wait()
        csb[u] = dot(place_t[pl.ds(other, HALF), :], retv[...]).astype(BF)
        remote(csb.at[u], crb.at[u], c_send, c_recv.at[u], sibling()).start()
        acc = dot(place_t[pl.ds(mine, HALF), :], retv[...])
        own[u] = acc + (dot_last(sdg[...], sg[wide, :]) + dot_last(sdu[...], su[wide, :]))

    def across(u):
        wait_for(crb.at[u], c_recv.at[u])
        own[u] = own[u] + crb[u].astype(F32)
        for o in (2, 1, 3):
            slot = pl.ds(pl.multiple_of(((x + o) % 4) * TD, TD), TD)
            xsb[u, o - 1] = own[u, slot, :].astype(BF)
            remote(xsb.at[u, o - 1], xrb.at[u, o - 1], x_send, x_recv.at[u], x_peer(o)).start()

    def finish(u):
        wait_for(xrb.at[u], x_recv.at[u])
        total = own[u, pl.ds(pl.multiple_of(x * TD, TD), TD), :]
        for o in range(3):
            total = total + xrb[u, o].astype(F32)
        fin[u] = total.astype(BF)
        wide = pl.ds(pl.multiple_of(u * UW, UW), UW)
        pltpu.make_async_copy(fin.at[u], out.at[:, wide], f_sem).start()

    @pl.loop(0, NU + 2)
    def _(t):
        @pl.when((t == 1) | (t == 3) | (t == 5))
        def _():
            unit = jnp.clip((t + 11) // 2, 6, 8)
            send_back(0, 4, unit, unit + 1)

        @pl.when(t < NU)
        def _():
            combine(jnp.minimum(t, NU - 1))

        @pl.when((t > 0) & (t <= NU))
        def _():
            across(jnp.clip(t - 1, 0, NU - 1))

        @pl.when(t > 1)
        def _():
            finish(jnp.maximum(t - 2, 0))

    wait_for(meta_all.at[pl.ds(0, 7)], m_send)
    wait_for(xg.at[:, pl.ds(0, 3 * TD), :], gx_send)
    wait_for(xg.at[:, pl.ds(0, 4 * TD), :], gc_send)
    wait_for(sb.at[:, pl.ds(0, ROWS - MSG), :], d_send)
    wait_for(ob.at[:, pl.ds(0, ROWS - MSG), :], r_send)
    wait_for(csb, c_send)
    wait_for(xsb, x_send)
    wait_for(fin, f_sem)


def hand_over(*refs):
    for j in range(5):
        refs[5 + j][...] = refs[j][...].reshape(refs[5 + j].shape)


def local(
    tokens,
    output_grad,
    chosen_experts,
    route_weights,
    gate_weight,
    up_weight,
    down_weight,
    gate_adapter_in,
    gate_adapter_out,
    up_adapter_in,
    up_adapter_out,
    shared_gate,
    shared_up,
    shared_down,
):
    any_spec = pl.BlockSpec(memory_space=pl.ANY)
    vmem = pl.BlockSpec(memory_space=pltpu.VMEM)
    rank = gate_adapter_in.shape[1]
    sff = shared_gate.shape[1]
    dma = pltpu.SemaphoreType.DMA
    shape = jax.ShapeDtypeStruct
    outs = pl.pallas_call(
        kernel,
        name="moe_backward",
        out_shape=(
            shape((TD, D), BF),
            shape((rank, D), F32),
            shape((rank, FF), F32),
            shape((rank, D), F32),
            shape((rank, FF), F32),
            shape((NA, ROWS, D), BF),
            shape((NA, ROWS, D), BF),
            shape((NU, ROWS, UW), BF),
            shape((NU, ROWS, UW), BF),
        ),
        in_specs=[any_spec] * 2
        + [vmem] * 2
        + [any_spec] * 3
        + [vmem] * 4
        + [any_spec] * 3,
        out_specs=(any_spec, vmem, vmem, vmem, vmem) + (any_spec,) * 4,
        scratch_shapes=[
            pltpu.VMEM((D, FF), BF),
            pltpu.VMEM((D, FF), BF),
            pltpu.VMEM((FF, D), BF),
            pltpu.VMEM((D, sff), BF),
            pltpu.VMEM((D, sff), BF),
            pltpu.VMEM((D, sff), BF),
            pltpu.VMEM((NB, 2, NPEER, TD), F32),
            pltpu.VMEM((NB, 2, NPEER, TD), F32),
            pltpu.VMEM((NA, NB * TD, D), BF),
            pltpu.VMEM((ROWS, NB * TD), BF),
            pltpu.VMEM((NB * TD, ROWS), BF),
            pltpu.VMEM((ROWS, TD), F32),
            pltpu.VMEM((ROWS, TD), F32),
            pltpu.VMEM((FIRST, GR, CW), F32),
            pltpu.VMEM((FIRST, GR, CW), BF),
            pltpu.VMEM((GR, D), BF),
            pltpu.VMEM((GR, D), BF),
            pltpu.VMEM((GR, FF), BF),
            pltpu.VMEM((GR, FF), BF),
            pltpu.VMEM((NU, GR, UW), BF),
            pltpu.VMEM((NA, MSG, D), BF),
            pltpu.VMEM((NU, MSG, UW), BF),
            pltpu.VMEM((HALF, sff), F32),
            pltpu.VMEM((HALF, sff), F32),
            pltpu.VMEM((HALF, sff), F32),
            pltpu.VMEM((HALF, sff), BF),
            pltpu.VMEM((HALF, sff), BF),
            pltpu.VMEM((ROWS, UW), BF),
            pltpu.VMEM((NU, HALF, UW), F32),
            pltpu.VMEM((NU, HALF, UW), BF),
            pltpu.VMEM((NU, HALF, UW), BF),
            pltpu.VMEM((NU, 3, TD, UW), BF),
            pltpu.VMEM((NU, 3, TD, UW), BF),
            pltpu.VMEM((NU, TD, UW), BF),
            dma((3,)),
            dma,
            dma,
            dma,
            dma,
            dma((len(PIECES),)),
            dma,
            dma((len(PIECES), 3)),
            dma,
            dma((len(PIECES),)),
            dma,
            dma,
            dma((4,)),
            dma,
            dma,
            dma,
            dma,
            dma((NU,)),
            dma,
            dma,
            dma,
            dma((NU,)),
            dma,
            dma((NU,)),
            dma,
        ],
        compiler_params=pltpu.CompilerParams(
            collective_id=0, has_side_effects=True, vmem_limit_bytes=62 << 20
        ),
    )(
        tokens,
        output_grad,
        chosen_experts.T,
        route_weights.T,
        gate_weight[0],
        up_weight[0],
        down_weight[0],
        gate_adapter_in[0],
        gate_adapter_out[0],
        up_adapter_in[0],
        up_adapter_out[0],
        shared_gate,
        shared_up,
        shared_down,
    )
    return pl.pallas_call(
        hand_over,
        name="hand_over",
        out_shape=(
            shape((TD, D), BF),
            shape((1, rank, D), F32),
            shape((1, rank, FF), F32),
            shape((1, rank, D), F32),
            shape((1, rank, FF), F32),
        ),
        in_specs=[vmem] * 5,
        out_specs=(vmem,) * 5,
    )(*outs[:5])


def solution(mesh):
    in_specs = (
        (P(("ep", "rep"), None),) * 4 + (P(("ep", "rep"), None, None),) * 7 + (P(None, "rep"),) * 3
    )
    out_specs = (P(("ep", "rep"), None),) + (P(("ep", "rep"), None, None),) * 4
    return jax.shard_map(
        local, mesh=mesh, in_specs=in_specs, out_specs=out_specs, check_vma=False
    )
```

```python
import jax
import jax.numpy as jnp
from jax import lax
from jax.experimental import pallas as pl
from jax.experimental.pallas import tpu as pltpu
from jax.sharding import PartitionSpec as P

MESH = pl.DeviceIdType.MESH
BF = jnp.bfloat16
F32 = jnp.float32

TD = 128
D = 2304
FF = 1024
CAP = 9
NB = 8
NPEER = 16
MSG = NB * CAP
ROWS = NPEER * MSG
GR = 4 * MSG
ND = 3
CW = D // ND
NA = 2
PIECES = ((0, 0, 1), (0, 1, 2), (0, 3, 3), (0, 6, 3), (1, 0, 3), (1, 3, 3), (1, 6, 3))
HALF = 4 * TD
UW = 256
NU = D // UW
FIRST = 2


def dot(a, b):
    return jnp.dot(a, b, preferred_element_type=F32)


def dot_last(a, b):
    return lax.dot_general(a, b, (((1,), (1,)), ((), ())), preferred_element_type=F32)


def dot_first(a, b):
    return lax.dot_general(a, b, (((0,), (0,)), ((), ())), preferred_element_type=F32)


def position():
    e, x = lax.axis_index("ep"), lax.axis_index("rep")
    return e // 8, (e // 2) % 4, e % 2, x


def peer(i, sign):
    z, y, c, x = position()
    oy = i % 4
    oz = (i % 4 + i // 4) % 4
    way = sign * (1 - 2 * c)
    zz = (z + way * oz + 4) % 4
    yy = (y + way * oy + 4) % 4
    return {"ep": (zz * 4 + yy) * 2 + c, "rep": x}


def x_peer(o):
    z, y, c, x = position()
    return {"ep": (z * 4 + y) * 2 + c, "rep": (x + o) % 4}


def member(o):
    z, y, c, x = position()
    return {"ep": (z * 4 + y) * 2 + (c + o // 4) % 2, "rep": (x + o) % 4}


def member_slot(o):
    z, y, c, x = position()
    return ((c + o // 4) % 2) * 4 + (x + o) % 4


def sibling():
    z, y, c, x = position()
    return {"ep": (z * 4 + y) * 2 + 1 - c, "rep": x}


def remote(src, dst, send, recv, device):
    return pltpu.make_async_remote_copy(
        src_ref=src,
        dst_ref=dst,
        send_sem=send,
        recv_sem=recv,
        device_id=device,
        device_id_type=MESH,
    )


def wait_for(ref, sem):
    pltpu.make_async_copy(ref, ref, sem).wait()


def kernel(
    tok,
    grd,
    chosen,
    route,
    gw_h,
    uw_h,
    dw_h,
    gin,
    gout,
    uin,
    uout,
    sg_h,
    su_h,
    sd_h,
    out,
    gin_g,
    gout_g,
    uin_g,
    uout_g,
    sb,
    rb,
    ob,
    ret,
    gw,
    uw,
    dw,
    sg,
    su,
    sd,
    meta,
    meta_all,
    xg,
    place,
    place_t,
    wsl,
    hits,
    tmp,
    stage,
    xb,
    gb,
    dg,
    du,
    outb,
    kept,
    back,
    sga,
    sua,
    sda,
    sdg,
    sdu,
    retv,
    own,
    csb,
    crb,
    xsb,
    xrb,
    fin,
    w_sem,
    s_sem,
    m_send,
    m_recv,
    m_own,
    own_sem,
    gx_send,
    gx_recv,
    gc_send,
    gc_recv,
    st_sem,
    d_send,
    d_recv,
    d_own,
    in_sem,
    o_sem,
    r_send,
    r_recv,
    r_own,
    rv_sem,
    c_send,
    c_recv,
    x_send,
    x_recv,
    f_sem,
):
    z, y, c, x = position()
    me = c * 4 + x

    barrier = pltpu.get_barrier_semaphore()

    @pl.loop(1, NPEER)
    def _(i):
        pl.semaphore_signal(barrier, inc=1, device_id=peer(i, 1), device_id_type=MESH)

    @pl.loop(1, 8)
    def _(o):
        pl.semaphore_signal(barrier, inc=1, device_id=member(o), device_id_type=MESH)

    weights = [(gw_h, gw), (uw_h, uw), (dw_h, dw)]
    shared = [(sg_h, sg), (su_h, su), (sd_h, sd)]

    def piece_of(p):
        a, first, width = PIECES[p]
        cols = pl.ds(first * UW, width * UW)
        return (grd if a else tok).at[:, cols], xg.at[a, pl.ds(me * TD, TD), cols]

    for p in range(len(PIECES)):
        src, dst = piece_of(p)
        pltpu.make_async_copy(src, dst, own_sem.at[p]).start()
    for h, v in shared:
        pltpu.make_async_copy(h, v, s_sem).start()
    for j, (h, v) in enumerate(weights):
        pltpu.make_async_copy(h, v, w_sem.at[j]).start()
    gin_g[...] = jnp.zeros_like(gin_g)
    gout_g[...] = jnp.zeros_like(gout_g)
    uin_g[...] = jnp.zeros_like(uin_g)
    uout_g[...] = jnp.zeros_like(uout_g)
    sga[...] = jnp.zeros_like(sga)
    sua[...] = jnp.zeros_like(sua)
    sda[...] = jnp.zeros_like(sda)

    row_i = lax.broadcasted_iota(jnp.int32, (TD, TD), 0)
    col_i = lax.broadcasted_iota(jnp.int32, (TD, TD), 1)
    group, chip = row_i >> 4, row_i & 15
    way = 1 - 2 * (group >> 2)
    zz = (z + way * ((chip & 3) + (chip >> 2)) + 8) & 3
    yy = (y + way * (chip & 3) + 8) & 3
    ids = (((zz * 4 + yy) * 2 + (group >> 2)) * 4) + (group & 3)
    picked = jnp.zeros((TD, TD), F32)
    weight = jnp.zeros((TD, TD), F32)
    for k in range(chosen.shape[0]):
        same = chosen[k : k + 1, :] == ids
        picked = jnp.where(same, 1.0, picked)
        weight = jnp.where(same, route[k : k + 1, :], weight)
    before = jnp.where(row_i < col_i, 1.0, 0.0).astype(BF)
    count = dot(picked.astype(BF), before)
    meta[:, 0] = jnp.where(picked > 0.0, count, -1.0).reshape(NB, NPEER, TD)
    meta[:, 1] = weight.reshape(NB, NPEER, TD)
    own_meta = pltpu.make_async_copy(meta.at[me], meta_all.at[me], m_own)
    own_meta.start()

    pl.semaphore_wait(barrier, NPEER - 1 + 7)

    @pl.loop(1, 8)
    def _(o):
        remote(meta.at[member_slot(o)], meta_all.at[me], m_send, m_recv, member(o)).start()

    for p in range(len(PIECES)):
        src, dst = piece_of(p)
        for o in (1, 3, 2):
            remote(src, dst, gx_send, gx_recv.at[p, o - 1], x_peer(o)).start()
        remote(src, dst, gc_send, gc_recv.at[p], sibling()).start()

    def message_rows():
        row = lax.broadcasted_iota(jnp.int32, (ROWS, TD), 0)
        lane = lax.broadcasted_iota(jnp.int32, (ROWS, TD), 1)
        nine = (row * 7282) >> 16
        slot = (row - CAP * nine).astype(F32)
        block = nine & 7
        spread = jnp.where(lane == block * NPEER + (nine >> 3), 1.0, 0.0).astype(BF)
        return spread, block, slot

    spread, block_of, slot_of = message_rows()

    own_meta.wait()
    wait_for(meta_all.at[pl.ds(0, 7)], m_recv)

    code = meta_all[:, 0].reshape(TD, TD).astype(BF)
    hit = jnp.where(dot(spread, code) == slot_of, 1.0, 0.0)
    hits[...] = hit
    for b in range(NB):
        place[:, b * TD : (b + 1) * TD] = jnp.where(block_of == b, hit, 0.0).astype(BF)

    wait_shared = [pltpu.make_async_copy(h, v, s_sem) for h, v in shared]
    for cp in wait_shared:
        cp.wait()

    mine = pl.multiple_of(c * HALF, HALF)
    other = pl.multiple_of((1 - c) * HALF, HALF)

    def rows_of(k):
        return pl.ds(pl.multiple_of(k * GR, 8), GR)

    def send_piece(a, cols, width, k, slot):
        filled = stage.at[slot, :, pl.ds(0, width)]
        cp = pltpu.make_async_copy(filled, sb.at[a, rows_of(k), cols], st_sem)
        cp.start()
        cp.wait()

        @pl.loop(0, 4)
        def _(j):
            i = k * 4 + j
            rows = pl.ds(pl.multiple_of(i * MSG, 8), MSG)

            @pl.when(i > 0)
            def _():
                remote(
                    sb.at[a, rows, cols], rb.at[a, rows, cols], d_send, d_recv.at[k], peer(i, 1)
                ).start()

            @pl.when(i == 0)
            def _():
                kept[a, :, cols] = stage[slot, 0:MSG, 0:width]
                pltpu.make_async_copy(kept.at[a, :, cols], rb.at[a, rows, cols], d_own).start()

    def scaled(acc, a, k):
        if isinstance(a, int) and a == 0:
            return acc.astype(BF)
        scale = jnp.where(a == 0, 1.0, wsl[rows_of(k), :][:, 0:1])
        return (acc * scale).astype(BF)

    def units(first, n):
        return pl.ds(pl.multiple_of((first + n) * UW, UW), UW)

    def first_groups(p, a, first, count):
        width = count * UW
        cols = pl.ds(pl.multiple_of(first * UW, UW), width)
        own_block = xg.at[a, pl.ds(me * TD, TD), cols]
        wait_for(own_block, own_sem.at[p])
        for o in (1, 3, 2):
            slot = pl.ds(pl.multiple_of((c * 4 + (x + 4 - o) % 4) * TD, TD), TD)
            block = xg.at[a, slot, cols]
            wait_for(block, gx_recv.at[p, o - 1])
            remote(block, block, gc_send, gc_recv.at[p], sibling()).start()

        @pl.loop(0, FIRST)
        def _(k):
            for n in range(count):
                tmp[k, :, n * UW : (n + 1) * UW] = dot(
                    place[rows_of(k), pl.ds(mine, HALF)], xg[a, pl.ds(mine, HALF), units(first, n)]
                )

        wait_for(xg.at[a, pl.ds(other, HALF), cols], gc_recv.at[p])

        @pl.loop(0, FIRST)
        def _(k):
            for n in range(count):
                here = slice(n * UW, (n + 1) * UW)
                acc = tmp[k, :, here] + dot(
                    place[rows_of(k), pl.ds(other, HALF)],
                    xg[a, pl.ds(other, HALF), units(first, n)],
                )
                stage[k, :, here] = scaled(acc, a, k)
            send_piece(a, cols, width, k, k)

        for n in range(count):
            block = xg[a, pl.ds(mine, HALF), units(first, n)]
            if a == 0:
                sga[...] += dot(block, sg[units(first, n), :])
                sua[...] += dot(block, su[units(first, n), :])
            else:
                sda[...] += dot(block, sd[units(first, n), :])

    first_groups(0, *PIECES[0])
    first_groups(1, *PIECES[1])

    @pl.loop(0, 2)
    def _(j):
        first_groups(2 + j, 0, 3 + 3 * j, 3)

    again = message_rows()[0]
    w_all = meta_all[:, 1].reshape(TD, TD)
    w_hi = w_all.astype(BF)
    left = w_all - w_hi.astype(F32)
    w_mid = left.astype(BF)
    w_lo = (left - w_mid.astype(F32)).astype(BF)
    w_row = (dot(again, w_hi) + dot(again, w_mid)) + dot(again, w_lo)
    wsl[...] = jnp.broadcast_to(jnp.sum(w_row * hits[...], axis=1, keepdims=True), (ROWS, TD))

    @pl.loop(0, 3)
    def _(j):
        first_groups(4 + j, 1, 3 * j, 3)

    s_gate, s_up, s_hid = sga[...], sua[...], sda[...]
    sig = jax.nn.sigmoid(s_gate)
    sdg[...] = (s_hid * s_up * sig * (1.0 + s_gate * (1.0 - sig))).astype(BF)
    sdu[...] = (s_hid * s_gate * sig).astype(BF)

    for j, (h, v) in enumerate(weights):
        pltpu.make_async_copy(h, v, w_sem.at[j]).wait()

    def late_piece(k, a, d):
        for n in range(3):
            acc = dot(place[rows_of(k), :], xg[a, :, units(3 * d, n)])
            stage[0, :, n * UW : (n + 1) * UW] = scaled(acc, a, k)
        send_piece(a, pl.ds(pl.multiple_of(d * CW, CW), CW), CW, k, 0)

    def fetch(k):
        pltpu.make_async_copy(rb.at[0, rows_of(k), :], xb, in_sem).start()
        pltpu.make_async_copy(rb.at[1, rows_of(k), :], gb, in_sem).start()
        wait_for(xb, in_sem)
        wait_for(gb, in_sem)

    def expert(k):
        low_gate = sum(dot_last(xb[:, d * CW : (d + 1) * CW], gin[:, d * CW : (d + 1) * CW]) for d in range(ND)).astype(BF)
        low_up = sum(dot_last(xb[:, d * CW : (d + 1) * CW], uin[:, d * CW : (d + 1) * CW]) for d in range(ND)).astype(BF)

        @pl.loop(0, FF // 256)
        def _(j):
            cols = pl.ds(pl.multiple_of(j * 256, 256), 256)
            gate = sum(dot(xb[:, d * CW : (d + 1) * CW], gw[d * CW : (d + 1) * CW, cols]) for d in range(ND))
            gate = gate + dot(low_gate, gout[:, cols])
            up = sum(dot(xb[:, d * CW : (d + 1) * CW], uw[d * CW : (d + 1) * CW, cols]) for d in range(ND))
            up = up + dot(low_up, uout[:, cols])
            hid = sum(dot_last(gb[:, d * CW : (d + 1) * CW], dw[cols, d * CW : (d + 1) * CW]) for d in range(ND))
            s = jax.nn.sigmoid(gate)
            dg[:, cols] = (hid * up * s * (1.0 + gate * (1.0 - s))).astype(BF)
            du[:, cols] = (hid * gate * s).astype(BF)

        dgv, duv = dg[...], du[...]
        low_dg = dot_last(dgv, gout[...]).astype(BF)
        low_du = dot_last(duv, uout[...]).astype(BF)
        gout_g[...] += dot_first(low_gate, dgv)
        uout_g[...] += dot_first(low_up, duv)
        for d in range(ND):
            cols = slice(d * CW, (d + 1) * CW)
            gin_g[:, cols] += dot_first(low_dg, xb[:, d * CW : (d + 1) * CW])
            uin_g[:, cols] += dot_first(low_du, xb[:, d * CW : (d + 1) * CW])

        @pl.loop(0, ND)
        def _(d):
            for n in range(3):
                rows = pl.ds(pl.multiple_of(d * CW + n * 256, 256), 256)
                acc = dot_last(dg[...], gw[rows, :]) + dot(low_dg, gin[:, rows])
                acc = acc + dot_last(du[...], uw[rows, :]) + dot(low_du, uin[:, rows])
                outb[3 * d + n] = acc.astype(BF)

    def store(k):
        @pl.loop(0, NU)
        def _(u):
            pltpu.make_async_copy(outb.at[u], ob.at[u, rows_of(k), :], o_sem).start()

        wait_for(outb, o_sem)

        @pl.when(k == 0)
        def _():
            back[...] = outb[:, 0:MSG, :]
            pltpu.make_async_copy(back, ret.at[:, pl.ds(0, MSG), :], r_own).start()

    def send_back(k_from, k_to, u_from, u_to):
        @pl.loop(u_from, u_to)
        def _(u):
            @pl.loop(4 * k_from, 4 * k_to)
            def _(i):
                rows = pl.ds(pl.multiple_of(i * MSG, 8), MSG)

                @pl.when(i > 0)
                def _():
                    remote(
                        ob.at[u, rows, :], ret.at[u, rows, :], r_send, r_recv.at[u], peer(i, -1)
                    ).start()

    @pl.loop(FIRST, 4)
    def _(k):
        @pl.loop(0, NA * ND)
        def _(p):
            late_piece(k, p // ND, p % ND)

    hit_t = hits[...].T
    block_row = ((lax.broadcasted_iota(jnp.int32, (TD, ROWS), 1) * 7282) >> 16) & 7
    for b in range(NB):
        place_t[b * TD : (b + 1) * TD, :] = jnp.where(block_row == b, hit_t, 0.0).astype(BF)

    @pl.loop(0, 4)
    def _(k):
        @pl.when(k == 0)
        def _():
            wait_for(rb.at[:, pl.ds(0, 3 * MSG), :], d_recv.at[0])
            wait_for(rb.at[:, pl.ds(0, MSG), :], d_own)

        @pl.when(k > 0)
        def _():
            wait_for(rb.at[:, pl.ds(0, GR), :], d_recv.at[k])

        fetch(k)
        expert(k)
        store(k)

        @pl.when(k < 3)
        def _():
            send_back(k, k + 1, 0, 3)

        @pl.when(k == 2)
        def _():
            send_back(0, 3, 3, 5)

        @pl.when(k == 3)
        def _():
            send_back(3, 4, 0, 5)
            send_back(0, 4, 5, 6)

    wait_for(ret.at[:, pl.ds(0, MSG), :], r_own)

    def combine(u):
        wide = pl.ds(pl.multiple_of(u * UW, UW), UW)
        wait_for(ret.at[u, pl.ds(0, ROWS - MSG), :], r_recv.at[u])
        cp = pltpu.make_async_copy(ret.at[u], retv, rv_sem)
        cp.start()
        cp.wait()
        csb[u] = dot(place_t[pl.ds(other, HALF), :], retv[...]).astype(BF)
        remote(csb.at[u], crb.at[u], c_send, c_recv.at[u], sibling()).start()
        acc = dot(place_t[pl.ds(mine, HALF), :], retv[...])
        own[u] = acc + (dot_last(sdg[...], sg[wide, :]) + dot_last(sdu[...], su[wide, :]))

    def across(u):
        wait_for(crb.at[u], c_recv.at[u])
        own[u] = own[u] + crb[u].astype(F32)
        for o in (2, 1, 3):
            slot = pl.ds(pl.multiple_of(((x + o) % 4) * TD, TD), TD)
            xsb[u, o - 1] = own[u, slot, :].astype(BF)
            remote(xsb.at[u, o - 1], xrb.at[u, o - 1], x_send, x_recv.at[u], x_peer(o)).start()

    def finish(u):
        wait_for(xrb.at[u], x_recv.at[u])
        total = own[u, pl.ds(pl.multiple_of(x * TD, TD), TD), :]
        for o in range(3):
            total = total + xrb[u, o].astype(F32)
        fin[u] = total.astype(BF)
        wide = pl.ds(pl.multiple_of(u * UW, UW), UW)
        pltpu.make_async_copy(fin.at[u], out.at[:, wide], f_sem).start()

    @pl.loop(0, NU + 2)
    def _(t):
        @pl.when((t == 1) | (t == 3) | (t == 5))
        def _():
            unit = jnp.clip((t + 11) // 2, 6, 8)
            send_back(0, 4, unit, unit + 1)

        @pl.when(t < NU)
        def _():
            combine(jnp.minimum(t, NU - 1))

        @pl.when((t > 0) & (t <= NU))
        def _():
            across(jnp.clip(t - 1, 0, NU - 1))

        @pl.when(t > 1)
        def _():
            finish(jnp.maximum(t - 2, 0))

    wait_for(meta_all.at[pl.ds(0, 7)], m_send)
    wait_for(xg.at[:, pl.ds(0, 3 * TD), :], gx_send)
    wait_for(xg.at[:, pl.ds(0, 4 * TD), :], gc_send)
    wait_for(sb.at[:, pl.ds(0, ROWS - MSG), :], d_send)
    wait_for(ob.at[:, pl.ds(0, ROWS - MSG), :], r_send)
    wait_for(csb, c_send)
    wait_for(xsb, x_send)
    wait_for(fin, f_sem)


def hand_over(*refs):
    for j in range(5):
        refs[5 + j][...] = refs[j][...].reshape(refs[5 + j].shape)


def local(
    tokens,
    output_grad,
    chosen_experts,
    route_weights,
    gate_weight,
    up_weight,
    down_weight,
    gate_adapter_in,
    gate_adapter_out,
    up_adapter_in,
    up_adapter_out,
    shared_gate,
    shared_up,
    shared_down,
):
    any_spec = pl.BlockSpec(memory_space=pl.ANY)
    vmem = pl.BlockSpec(memory_space=pltpu.VMEM)
    rank = gate_adapter_in.shape[1]
    sff = shared_gate.shape[1]
    dma = pltpu.SemaphoreType.DMA
    shape = jax.ShapeDtypeStruct
    outs = pl.pallas_call(
        kernel,
        name="moe_backward",
        out_shape=(
            shape((TD, D), BF),
            shape((rank, D), F32),
            shape((rank, FF), F32),
            shape((rank, D), F32),
            shape((rank, FF), F32),
            shape((NA, ROWS, D), BF),
            shape((NA, ROWS, D), BF),
            shape((NU, ROWS, UW), BF),
            shape((NU, ROWS, UW), BF),
        ),
        in_specs=[any_spec] * 2
        + [vmem] * 2
        + [any_spec] * 3
        + [vmem] * 4
        + [any_spec] * 3,
        out_specs=(any_spec, vmem, vmem, vmem, vmem) + (any_spec,) * 4,
        scratch_shapes=[
            pltpu.VMEM((D, FF), BF),
            pltpu.VMEM((D, FF), BF),
            pltpu.VMEM((FF, D), BF),
            pltpu.VMEM((D, sff), BF),
            pltpu.VMEM((D, sff), BF),
            pltpu.VMEM((D, sff), BF),
            pltpu.VMEM((NB, 2, NPEER, TD), F32),
            pltpu.VMEM((NB, 2, NPEER, TD), F32),
            pltpu.VMEM((NA, NB * TD, D), BF),
            pltpu.VMEM((ROWS, NB * TD), BF),
            pltpu.VMEM((NB * TD, ROWS), BF),
            pltpu.VMEM((ROWS, TD), F32),
            pltpu.VMEM((ROWS, TD), F32),
            pltpu.VMEM((FIRST, GR, CW), F32),
            pltpu.VMEM((FIRST, GR, CW), BF),
            pltpu.VMEM((GR, D), BF),
            pltpu.VMEM((GR, D), BF),
            pltpu.VMEM((GR, FF), BF),
            pltpu.VMEM((GR, FF), BF),
            pltpu.VMEM((NU, GR, UW), BF),
            pltpu.VMEM((NA, MSG, D), BF),
            pltpu.VMEM((NU, MSG, UW), BF),
            pltpu.VMEM((HALF, sff), F32),
            pltpu.VMEM((HALF, sff), F32),
            pltpu.VMEM((HALF, sff), F32),
            pltpu.VMEM((HALF, sff), BF),
            pltpu.VMEM((HALF, sff), BF),
            pltpu.VMEM((ROWS, UW), BF),
            pltpu.VMEM((NU, HALF, UW), F32),
            pltpu.VMEM((NU, HALF, UW), BF),
            pltpu.VMEM((NU, HALF, UW), BF),
            pltpu.VMEM((NU, 3, TD, UW), BF),
            pltpu.VMEM((NU, 3, TD, UW), BF),
            pltpu.VMEM((NU, TD, UW), BF),
            dma((3,)),
            dma,
            dma,
            dma,
            dma,
            dma((len(PIECES),)),
            dma,
            dma((len(PIECES), 3)),
            dma,
            dma((len(PIECES),)),
            dma,
            dma,
            dma((4,)),
            dma,
            dma,
            dma,
            dma,
            dma((NU,)),
            dma,
            dma,
            dma,
            dma((NU,)),
            dma,
            dma((NU,)),
            dma,
        ],
        compiler_params=pltpu.CompilerParams(
            collective_id=0, has_side_effects=True, vmem_limit_bytes=62 << 20
        ),
    )(
        tokens,
        output_grad,
        chosen_experts.T,
        route_weights.T,
        gate_weight[0],
        up_weight[0],
        down_weight[0],
        gate_adapter_in[0],
        gate_adapter_out[0],
        up_adapter_in[0],
        up_adapter_out[0],
        shared_gate,
        shared_up,
        shared_down,
    )
    return pl.pallas_call(
        hand_over,
        name="hand_over",
        out_shape=(
            shape((TD, D), BF),
            shape((1, rank, D), F32),
            shape((1, rank, FF), F32),
            shape((1, rank, D), F32),
            shape((1, rank, FF), F32),
        ),
        in_specs=[vmem] * 5,
        out_specs=(vmem,) * 5,
    )(*outs[:5])


def solution(mesh):
    in_specs = (
        (P(("ep", "rep"), None),) * 4 + (P(("ep", "rep"), None, None),) * 7 + (P(None, "rep"),) * 3
    )
    out_specs = (P(("ep", "rep"), None),) + (P(("ep", "rep"), None, None),) * 4
    return jax.shard_map(
        local, mesh=mesh, in_specs=in_specs, out_specs=out_specs, check_vma=False
    )
```
